256 devices in a mesh: seq: 16 (over z, core), dp: 16 (over y, x).
Axes of the slice: x: 4, y: 4, z: 8, core: 2. Of those that a mesh axis runs over, the one named last changes fastest.
Arguments:
- queries: bfloat16 [16, 2048, 1280], P('dp', 'seq'), may hold values from -43 to 43
- key_rows: bfloat16 [16, 2048, 1280], P('dp', 'seq'), may hold values from -7 to 7
- value_rows: bfloat16 [16, 2048, 1280], P('dp', 'seq'), may hold values from -6 to 6
- resid_in: bfloat16 [16, 2048, 1280], P('dp', 'seq'), may hold values from -6 to 6
- llm_grad: bfloat16 [16, 3072, 1280], P('dp', 'seq'), may hold values from -6 to 6
- vision_slot: int32 [16, 3072], P('dp', 'seq'), may hold values from -1 to 2047, as said below
- window_mask: int32 [16, 32, 2], P('dp', 'seq'), may hold values from 0 to 1, as said below
- w_up: bfloat16 [1280, 2560], P('dp'), may hold values from -0.15625 to 0.15625
- w_down: bfloat16 [2560, 1280], P('dp'), may hold values from -0.125 to 0.125
- norm_gain: bfloat16 [1280], P('dp'), may hold values from 0.25 to 1.75
Outputs:
- grad_query: bfloat16 [16, 2048, 1280], P('dp', 'seq')
- grad_key: bfloat16 [16, 2048, 1280], P('dp', 'seq')
- grad_value: bfloat16 [16, 2048, 1280], P('dp', 'seq')
- grad_resid: bfloat16 [16, 2048, 1280], P('dp', 'seq')
- grad_up: bfloat16 [1280, 2560], P('seq', 'dp')
- grad_down: bfloat16 [2560, 1280], P('seq', 'dp')
- grad_gain: float32 [1280], replicated
The draws below stay inside these ranges and needn't reach their ends.
Inputs may be any that keep to these rules, and one draw needn't show every extreme that they name: `vision_slot`: -1 marks a text position; every vision token of a batch stands at exactly one position. Positions come in aligned runs of 16: each run is text or the 16 consecutive vision tokens of one tile, in order. Each language-model shard holds exactly 8 tiles, and at most 32 vision tokens of one owner; in every batch, for every owner, some shard holds exactly 32 of that owner's vision tokens. `window_mask`: each owner's 2 blocks are split into images of one or more consecutive blocks; a block attends to exactly the blocks of its own image, itself included (entry i % 2 of row i is 1).
All inputs are finite; a program needn't handle non-finite values.
Results may differ from the reference program's by a relative error of at most 0.023.
Values may be sent and summed in bfloat16 or wider, within the bound.
A program may use at most 128 MiB of HBM per device.

```python
import math
import jax
import jax.numpy as jnp
from jax import lax

HEADS = 16
HDIM = 80
D = 1280
FF = 2560
BLK = 64
PIECE = 16
TOK_DEV = 128
NBD = 2
NPIECE = 8
L_DEV = 192
VISION = 2048
LLM_LEN = 3072
BATCHES = 16
N_SEQ = 16


def query_key_pair(key):
    base = jax.random.fold_in(key, 11)
    query_key, other_key = jax.random.split(base)
    shape = (BATCHES, VISION, D)
    query_out = jnp.clip(jax.random.normal(query_key, shape, jnp.float32), -6.0, 6.0)
    key_out = jnp.clip(jax.random.normal(other_key, shape, jnp.float32), -6.0, 6.0)
    return (query_out, key_out)


def draw_queries(key, part):
    return query_key_pair(key)[0].astype(jnp.bfloat16)


def draw_key_rows(key, part):
    return query_key_pair(key)[1].astype(jnp.bfloat16)


def draw_vision_slot(key, part):
    slot_count = L_DEV // PIECE

    def one_batch(batch_key):
        order_key, place_key = jax.random.split(batch_key)
        order = jax.random.permutation(order_key, N_SEQ)
        tile_index = jnp.arange(NPIECE)
        shifts = jnp.where(tile_index == 0, order[0], order[(tile_index - 1) % N_SEQ])
        sender = jnp.arange(N_SEQ)[:, None]
        owner = (sender - shifts[None, :]) % N_SEQ
        first = owner * TOK_DEV + tile_index[None, :] * PIECE
        layout = jax.vmap(lambda one_key: jax.random.permutation(one_key, slot_count))(jax.random.split(place_key, N_SEQ))
        clipped = jnp.minimum(layout, NPIECE - 1)
        starts = jnp.where(layout < NPIECE, jnp.take_along_axis(first, clipped, axis=1), -1)
        offsets = jnp.arange(PIECE)
        values = jnp.where(starts[:, :, None] >= 0, starts[:, :, None] + offsets[None, None, :], -1)
        return values.reshape(N_SEQ * L_DEV).astype(jnp.int32)
    return jax.vmap(one_batch)(jax.random.split(jax.random.fold_in(key, 23), BATCHES))


def draw_window_mask(key, part):
    cut_key = jax.random.fold_in(key, 37)
    cuts = jax.random.randint(cut_key, (BATCHES, N_SEQ, NBD), 0, 2)
    cuts = jnp.where(jnp.arange(NBD)[None, None, :] == 0, 0, cuts)
    image = jnp.cumsum(cuts, axis=2)
    allowed = image[:, :, :, None] == image[:, :, None, :]
    return allowed.astype(jnp.int32).reshape(BATCHES, N_SEQ * NBD, NBD)


def spiked(values, stream_key, source, target, shards_of, factor):
    owner, partner = [(jnp.arange(values.shape[axis_at]) // (values.shape[axis_at] // shards_of)).reshape([-1 if axis == axis_at else 1 for axis in range(values.ndim)]) for axis_at in (source, target)]
    chosen = jax.random.permutation(stream_key, shards_of)[partner]
    strong = (owner == chosen) | (owner == (partner + shards_of // 2) % shards_of)
    return jnp.where(strong, factor * values, values)


def level_of(own_key, dims, shards, least, largest):
    loudness = 1.0
    for dim, shards_of in shards:
        heights = jax.random.uniform(jax.random.fold_in(jax.random.fold_in(own_key, 6), dim), (shards_of,), jnp.float32, least / len(shards), largest / len(shards))
        loudness = loudness * jnp.repeat(jnp.exp(heights), dims[dim] // shards_of).reshape((-1,) + (1,) * (len(dims) - 1 - dim))
    return loudness


def bell_draw(key, dims, spread, limit, shards=(), held_as=jnp.bfloat16):
    values = spread * jax.random.normal(key, dims, jnp.float32)
    if shards:
        values = values * level_of(key, dims, shards, -0.22, 0.18)
    return jnp.clip(values, -limit, limit).astype(held_as)


def gaussian_with(stream_key, extent, width, limit, shards, heavy, kind=jnp.bfloat16):
    result = width * jax.random.normal(stream_key, extent, jnp.float32)
    if shards:
        result = result * level_of(stream_key, extent, shards, -0.22, 0.18)
    return jnp.clip(spiked(result, jax.random.fold_in(stream_key, 3), *heavy), -limit, limit).astype(kind)


def setup_inputs(seed: int = 0) -> dict:
    splits = jax.random.split(jax.random.key(seed), 11)
    return {
        "queries": draw_queries(jax.random.fold_in(splits[10], 71), 0),
        "key_rows": draw_key_rows(jax.random.fold_in(splits[10], 71), 0),
        "value_rows": bell_draw(splits[2], (BATCHES, VISION, D), 1.0, 6.0, ((0, 16), (1, 16))),
        "resid_in": bell_draw(splits[3], (BATCHES, VISION, D), 1.0, 6.0, ((0, 16), (1, 16))),
        "llm_grad": gaussian_with(splits[4], (BATCHES, LLM_LEN, D), 1.0, 6.0, ((0, 16), (1, 16)), (1, 2, 16, 2.0)),
        "vision_slot": draw_vision_slot(jax.random.fold_in(splits[10], 71), 0),
        "window_mask": draw_window_mask(jax.random.fold_in(splits[10], 71), 0),
        "w_up": bell_draw(splits[7], (D, FF), D ** -0.5, 0.15625, ((0, 16),)),
        "w_down": bell_draw(splits[8], (FF, D), FF ** -0.5, 0.125, ((0, 16),)),
        "norm_gain": jnp.clip(1.0 + 0.15 * jax.random.normal(splits[9], (D,), jnp.float32), 0.25, 1.75).astype(jnp.bfloat16),
    }


def rounded(value):
    return lax.optimization_barrier(value.astype(jnp.bfloat16))

def contract(left, right, left_dim, right_dim):
    return lax.dot_general(left, right, (((left_dim,), (right_dim,)), ((), ())), preferred_element_type=jnp.float32)

def owner_pass(query, key_block, value_block, resid, grad_rows, window_mask, up_full, down_full, gain_full):
    tokens = query.shape[0]
    att_scale = 1.0 / math.sqrt(HDIM)
    best = lax.Precision.HIGHEST
    allowed = jnp.repeat(jnp.repeat(window_mask > 0, BLK, axis=0), BLK, axis=1)
    q_heads = query.astype(jnp.float32).reshape(tokens, HEADS, HDIM)
    k_heads = key_block.astype(jnp.float32).reshape(tokens, HEADS, HDIM)
    v_heads = value_block.astype(jnp.float32).reshape(tokens, HEADS, HDIM)
    scores = jnp.einsum('qhd,khd->hqk', q_heads, k_heads, precision=best) * att_scale
    masked = jnp.where(allowed[None], scores, -jnp.inf)
    highest = lax.optimization_barrier(jnp.max(masked, axis=2, keepdims=True))
    exp_terms = jnp.where(allowed[None], jnp.exp(masked - highest), 0.0)
    attn_probs = exp_terms / lax.optimization_barrier(jnp.sum(exp_terms, axis=2, keepdims=True))
    probs_low = rounded(attn_probs)
    attn_heads = rounded(jnp.einsum('hqk,khd->qhd', probs_low.astype(jnp.float32), v_heads, precision=best))
    attn_out = attn_heads.reshape(tokens, HEADS * HDIM)
    hidden = resid.astype(jnp.float32) + attn_out.astype(jnp.float32)
    center = lax.optimization_barrier(jnp.mean(hidden, axis=1, keepdims=True))
    variance = lax.optimization_barrier(jnp.mean(jnp.square(hidden - center), axis=1, keepdims=True))
    inverse = lax.rsqrt(variance + 1e-06)
    normal_unit = (hidden - center) * inverse
    gain_wide = gain_full.astype(jnp.float32)
    normed = rounded(normal_unit * gain_wide)
    pre_act = jnp.dot(normed, up_full, preferred_element_type=jnp.float32)
    sig_gate = jax.nn.sigmoid(1.702 * pre_act)
    act_low = rounded(pre_act * sig_gate)
    d_act = contract(grad_rows, down_full, 1, 1)
    d_pre = rounded(d_act * (sig_gate + 1.702 * pre_act * sig_gate * (1.0 - sig_gate)))
    d_normed = contract(d_pre, up_full, 1, 1)
    gain_term = lax.optimization_barrier(jnp.sum(d_normed * normal_unit, axis=0))
    d_unit = d_normed * gain_wide
    d_hidden = inverse * (d_unit - lax.optimization_barrier(jnp.mean(d_unit, axis=1, keepdims=True)) - normal_unit * lax.optimization_barrier(jnp.mean(d_unit * normal_unit, axis=1, keepdims=True)))
    grad_resid = rounded(grad_rows.astype(jnp.float32) + d_hidden)
    grad_heads = grad_resid.astype(jnp.float32).reshape(tokens, HEADS, HDIM)
    grad_value = rounded(jnp.einsum('hqk,qhd->khd', probs_low.astype(jnp.float32), grad_heads, precision=best))
    d_probs = jnp.einsum('qhd,khd->hqk', grad_heads, v_heads, precision=best)
    delta = jnp.einsum('qhd,qhd->hq', grad_heads, attn_heads.astype(jnp.float32), precision=best)
    d_scores = rounded(attn_probs * (d_probs - delta[:, :, None]) * att_scale)
    grad_query = rounded(jnp.einsum('hqk,khd->qhd', d_scores.astype(jnp.float32), k_heads, precision=best))
    grad_key = rounded(jnp.einsum('hqk,qhd->khd', d_scores.astype(jnp.float32), q_heads, precision=best))
    down_term = contract(act_low, grad_rows, 0, 0)
    up_term = contract(normed, d_pre, 0, 0)
    flat = (tokens, HEADS * HDIM)
    return (grad_query.reshape(flat), grad_key.reshape(flat), grad_value.reshape(flat), grad_resid, up_term, down_term, gain_term)

def reference(queries, key_rows, value_rows, resid_in, llm_grad, vision_slot, window_mask, w_up, w_down, norm_gain):

    def batch_step(totals, batch):
        query, key_block, value_block, resid, llm_rows, slot_ids, mask_rows = batch
        target = jnp.where(slot_ids >= 0, slot_ids, VISION).astype(jnp.int32)
        grad_rows = jnp.zeros((VISION, D), jnp.bfloat16).at[target].set(llm_rows, mode='drop')
        per_owner = (query.reshape(N_SEQ, TOK_DEV, D), key_block.reshape(N_SEQ, TOK_DEV, D), value_block.reshape(N_SEQ, TOK_DEV, D), resid.reshape(N_SEQ, TOK_DEV, D), grad_rows.reshape(N_SEQ, TOK_DEV, D), mask_rows.reshape(N_SEQ, NBD, NBD))

        def owner_step(sums, owner):
            results = owner_pass(owner[0], owner[1], owner[2], owner[3], owner[4], owner[5], w_up, w_down, norm_gain)
            up_sum = sums[0] + rounded(results[4]).astype(jnp.float32)
            down_sum = sums[1] + rounded(results[5]).astype(jnp.float32)
            gain_sum = sums[2] + results[6]
            return ((up_sum, down_sum, gain_sum), (results[0], results[1], results[2], results[3]))
        start = (jnp.zeros((D, FF), jnp.float32), jnp.zeros((FF, D), jnp.float32), jnp.zeros((D,), jnp.float32))
        inner, grads = lax.scan(owner_step, start, per_owner)
        up_total = totals[0] + rounded(inner[0]).astype(jnp.float32)
        down_total = totals[1] + rounded(inner[1]).astype(jnp.float32)
        gain_total = totals[2] + inner[2]
        shaped = (grads[0].reshape(VISION, D), grads[1].reshape(VISION, D), grads[2].reshape(VISION, D), grads[3].reshape(VISION, D))
        return ((up_total, down_total, gain_total), shaped)
    start = (jnp.zeros((D, FF), jnp.float32), jnp.zeros((FF, D), jnp.float32), jnp.zeros((D,), jnp.float32))
    final, grads = lax.scan(batch_step, start, (queries, key_rows, value_rows, resid_in, llm_grad, vision_slot, window_mask))
    factor = 1.0 / math.sqrt(BATCHES * VISION)
    return (grads[0], grads[1], grads[2], grads[3], (final[0] * factor).astype(jnp.bfloat16), (final[1] * factor).astype(jnp.bfloat16), final[2] * factor)
```

```python
import math

import jax
import jax.numpy as jnp
from jax import lax
from jax.experimental import pallas as pl
from jax.experimental.pallas import tpu as pltpu
from jax.sharding import PartitionSpec as P

HEADS = 16
HDIM = 80
BLK = 64
PIECE = 16
D = 1280
FF = 2560
TOK = 128
NS = 16
ND = 16
CAP = 32
NY, NX, NZ = 4, 4, 8
FQ = FF // NY
ROWS_DP = D // ND
FF_DP = FF // ND
WIN = 256
MESH = pl.DeviceIdType.MESH
BF = jnp.bfloat16
F32 = jnp.float32


def mm(left, right, left_dim, right_dim):
    return lax.dot_general(
        left, right, (((left_dim,), (right_dim,)), ((), ())), preferred_element_type=F32
    )


def window_start(z):
    return pl.multiple_of(128 * ((5 * z) // 4), 128)


def kernel(
    rows_ref,
    ids_ref,
    wup_ref,
    wdown_ref,
    unit_ref,
    gain_ref,
    dn_ref,
    grows_ref,
    gain_out_ref,
    ggain_ref,
    up_ref,
    down_ref,
    rr,
    ri,
    gr,
    wu,
    wd,
    ra,
    la,
    gate,
    dns,
    dnr,
    gt,
    cr,
    xs,
    xr,
    zs,
    zr,
    fs,
    fu,
    fd,
    gp,
    gs1,
    gp2,
    gs2,
    s_loc,
    s_rr,
    r_rr,
    s_ri,
    r_ri,
    s_gr,
    r_gr,
    s_wy,
    r_wy,
    s_wx,
    r_wx,
    s_rl,
    r_rl,
    s_na,
    r_na,
    s_ga,
    r_ga,
    s_dn,
    r_dn,
    s_c,
    r_c,
    s_x,
    r_x,
    s_z,
    r_z,
    s_f,
    r_f,
    s_g1,
    r_g1,
    s_g2,
    r_g2,
):
    s = lax.axis_index("seq")
    d = lax.axis_index("dp")
    z, c = s // 2, s % 2
    y, x = d // NX, d % NX

    def remote(src, dst, send, recv, to_s, to_d):
        return pltpu.make_async_remote_copy(
            src_ref=src,
            dst_ref=dst,
            send_sem=send,
            recv_sem=recv,
            device_id=(to_s, to_d),
            device_id_type=MESH,
        )

    def y_peer(k):
        return ((y + k) % NY) * NX + x

    def x_peer(k):
        return y * NX + (x + k) % NX

    barrier = pltpu.get_barrier_semaphore()
    for k in range(1, NS):
        pl.semaphore_signal(barrier, inc=1, device_id=((s + k) % NS, d), device_id_type=MESH)
    for k in range(1, ND):
        pl.semaphore_signal(barrier, inc=1, device_id=(s, (d + k) % ND), device_id_type=MESH)
    from_s = 2 * (d // 2) + 1
    own_final = jnp.logical_and(from_s == s, s == d)

    @pl.when(jnp.logical_not(own_final))
    def _():
        pl.semaphore_signal(barrier, inc=1, device_id=(from_s, s), device_id_type=MESH)

    pl.semaphore_wait(barrier, NS + ND - 2 + 2 * c - jnp.where(own_final, 1, 0))

    def gain_copy(k):
        return remote(gain_ref, gr.at[d], s_gr.at[k], r_gr.at[k], s, (d + k) % ND)

    for k in range(1, ND):
        gain_copy(k).start()

    def row_copy(k):
        to = (s + k) % NS
        return remote(rows_ref.at[to], rr.at[s], s_rr.at[k], r_rr.at[k], to, d)

    def id_copy(k):
        to = (s + k) % NS
        return remote(ids_ref.at[to], ri.at[s], s_ri.at[k], r_ri.at[k], to, d)

    for k in range(1, NS):
        id_copy(k).start()
        row_copy(k).start()
    own_rows = pltpu.make_async_copy(rows_ref.at[s], rr.at[s], s_loc.at[0])
    own_ids = pltpu.make_async_copy(ids_ref.at[s], ri.at[s], s_loc.at[1])
    own_rows.start()
    own_ids.start()

    def quarter(q):
        return wup_ref.at[:, pl.ds(pl.multiple_of(q * FQ, 128), FQ)]

    def wy_copy(k):
        return remote(
            quarter((y + k) % NY), wu.at[y, x], s_wy.at[k], r_wy.at[k], s, y_peer(k)
        )

    def ux_copy(k):
        return remote(wu.at[:, x], wu.at[:, x], s_wx.at[k], r_wx.at[k], s, x_peer(k))

    def dx_copy(k):
        return remote(wd.at[x], wd.at[x], s_wx.at[k], r_wx.at[k], s, x_peer(k))

    def ul_copy(k):
        at = (x + NX - k) % NX
        return remote(wu.at[:, at], wu.at[:, at], s_rl.at[k], r_rl.at[k], s + 1, d)

    def dl_copy(k):
        at = (x + NX - k) % NX
        return remote(wd.at[at], wd.at[at], s_rl.at[k], r_rl.at[k], s - 1, d)

    own_up = pltpu.make_async_copy(quarter(y), wu.at[y, x], s_loc.at[2])
    own_down = pltpu.make_async_copy(wdown_ref, wd.at[x], s_loc.at[3])

    @pl.when(c == 0)
    def _():
        for k in range(1, NY):
            wy_copy(k).start()
        own_up.start()
        own_up.wait()

    @pl.when(c == 1)
    def _():
        own_down.start()
        own_down.wait()
        for k in range(1, NX):
            dx_copy(k).start()
        dl_copy(0).start()

    gr[d] = gain_ref[...]
    for k in range(1, ND):
        gain_copy(k).wait_recv()
    gain_full = jnp.sum(gr[...], axis=0)
    gain_out_ref[...] = gain_full
    ra[0, y] = (unit_ref[...] * gain_full).astype(BF)

    def na_copy(k):
        return remote(ra.at[0, y], ra.at[0, y], s_na.at[k], r_na.at[k], s, y_peer(k))

    for k in range(1, NY):
        na_copy(k).start()

    @pl.when(c == 0)
    def _():
        for k in range(1, NY):
            wy_copy(k).wait_recv()
        for k in range(1, NX):
            ux_copy(k).start()
        ul_copy(0).start()
        for k in (1, 3, 2):
            ux_copy(k).wait_recv()
            ul_copy(k).start()
        for k in range(NX):
            dl_copy(k).wait_recv()

    @pl.when(c == 1)
    def _():
        for k in (1, 3, 2):
            dx_copy(k).wait_recv()
            dl_copy(k).start()
        for k in range(NX):
            ul_copy(k).wait_recv()

    for k in range(1, NY):
        na_copy(k).wait_recv()

    half = 2 * TOK

    def up_step(i, carry):
        rows = pl.ds(pl.multiple_of(i * half, half), half)
        pre = mm(
            ra[0, pl.ds(2 * i, 2)].reshape(half, D), wu[...].reshape(D, FQ), 1, 0
        )
        sig = jax.nn.sigmoid(1.702 * pre)
        la[1, rows, :] = (pre * sig).astype(BF)
        gate[rows, :] = sig + 1.702 * pre * sig * (1.0 - sig)
        return carry

    lax.fori_loop(0, 2, up_step, 0)

    own_rows.wait()
    own_ids.wait()
    for k in range(1, NS):
        id_copy(k).wait_recv()
        row_copy(k).wait_recv()
    total = None
    token = lax.broadcasted_iota(jnp.int32, (TOK, 128), 0)
    for j in range(4):
        ids = jnp.max(ri[4 * j : 4 * j + 4], axis=0)
        place = jnp.where(token == ids, 1.0, 0.0).astype(BF)
        part = mm(place, rr[4 * j : 4 * j + 4].reshape(4 * CAP, D), 1, 0)
        total = part if total is None else total + part
    own_grad = total.astype(BF)
    ra[1, y] = own_grad
    grows_ref[...] = own_grad

    def ga_copy(k):
        return remote(ra.at[1, y], ra.at[1, y], s_ga.at[k], r_ga.at[k], s, y_peer(k))

    for k in range(1, NY):
        ga_copy(k).start()
    for k in range(1, NY):
        ga_copy(k).wait_recv()

    def down_step(i, carry):
        rows = pl.ds(pl.multiple_of(i * half, half), half)
        d_act = mm(
            ra[1, pl.ds(2 * i, 2)].reshape(half, D), wd[...].reshape(FQ, D), 1, 1
        )
        la[0, rows, :] = (d_act * gate[rows, :]).astype(BF)
        return carry

    lax.fori_loop(0, 2, down_step, 0)

    def norm_step(i, acc):
        rows = pl.ds(pl.multiple_of(i * half, half), half)
        part = mm(la[0, rows, :], wu[...].reshape(D, FQ), 1, 1)
        dns[pl.ds(2 * i, 2)] = part.astype(BF).reshape(2, TOK, D)
        normed = ra[0, pl.ds(2 * i, 2)].reshape(half, D).astype(F32)
        return acc + jnp.sum(part * normed, axis=0, keepdims=True)

    gp[...] = lax.fori_loop(0, 2, norm_step, jnp.zeros((1, D), F32))

    def dn_copy(k):
        to = (y + k) % NY
        return remote(dns.at[to], dnr.at[y], s_dn.at[k], r_dn.at[k], s, to * NX + x)

    for k in range(1, NY):
        dn_copy(k).start()

    def g1_copy(k):
        return remote(gp, gs1.at[s], s_g1.at[k], r_g1.at[k], (s + k) % NS, d)

    for k in range(1, NS):
        g1_copy(k).start()

    def weight_grad(part):
        def step(i, carry):
            lanes = pl.ds(pl.multiple_of(i * 128, 128), 128)
            value = mm(la[part, :, lanes], ra[part].reshape(NY * TOK, D), 0, 0)
            gt[part, pl.ds(pl.multiple_of(i * 128, 128), 128), :] = value.astype(BF)
            return carry

        lax.fori_loop(0, FQ // 128, step, 0)

    c_copy = remote(gt.at[1 - c], cr, s_c.at[0], r_c.at[0], s + 1 - 2 * c, d)
    weight_grad(1 - c)
    c_copy.start()
    weight_grad(c)
    c_copy.wait_recv()

    def c_sum(i, carry):
        rows = pl.ds(pl.multiple_of(i * 32, 32), 32)
        xs[rows, :] = (gt[c, rows, :].astype(F32) + cr[rows, :].astype(F32)).astype(BF)
        return carry

    lax.fori_loop(0, FQ // 32, c_sum, 0)

    def block(i):
        return pl.ds(pl.multiple_of(i * FF_DP, FF_DP), FF_DP)

    def x_copy(k):
        to = (x + k) % NX
        return remote(xs.at[block(to)], xr.at[x], s_x.at[k], r_x.at[k], s, y * NX + to)

    for k in range(1, NX):
        x_copy(k).start()

    gs1[s] = gp[...]
    for k in range(1, NS):
        g1_copy(k).wait_recv()
    gp2[...] = jnp.sum(gs1[...], axis=0)

    def g2_copy(k):
        return remote(gp2, gs2.at[d], s_g2.at[k], r_g2.at[k], s, (d + k) % ND)

    for k in range(1, ND):
        g2_copy(k).start()

    dnr[y] = dns[y]
    for k in range(1, NY):
        dn_copy(k).wait_recv()

    def dn_sum(i, carry):
        rows = pl.ds(pl.multiple_of(i * 32, 32), 32)
        dn_ref[rows, :] = jnp.sum(dnr[:, rows, :].astype(F32), axis=0)
        return carry

    lax.fori_loop(0, TOK // 32, dn_sum, 0)

    for k in range(1, NX):
        x_copy(k).wait_recv()
    xr[x] = xs[block(x), :]

    def x_sum(i, carry):
        rows = pl.ds(pl.multiple_of(i * 32, 32), 32)
        zs[rows, :] = jnp.sum(xr[:, rows, :].astype(F32), axis=0).astype(BF)
        return carry

    lax.fori_loop(0, FF_DP // 32, x_sum, 0)

    def z_copy(k):
        to = (z + k) % NZ
        return remote(
            zs.at[:, pl.ds(window_start(to), WIN)],
            zr.at[z],
            s_z.at[k],
            r_z.at[k],
            2 * to + c,
            d,
        )

    for k in range(1, NZ):
        z_copy(k).start()
    zr[z] = zs[:, pl.ds(window_start(z), WIN)]

    gs2[d] = gp2[...]
    for k in range(1, ND):
        g2_copy(k).wait_recv()
    factor = 1.0 / math.sqrt(NS * ND * TOK)
    ggain_ref[...] = jnp.sum(gs2[...], axis=0) * factor / gain_out_ref[...]

    for k in range(1, NZ):
        z_copy(k).wait_recv()
    fs[...] = (jnp.sum(zr[...].astype(F32), axis=0) * factor).astype(BF)

    u_copy = remote(fs, fu, s_f.at[0], r_f.at[0], s + 1, d)
    d0_copy = remote(fs, fd, s_f.at[1], r_f.at[1], d, 2 * z)
    d1_copy = remote(fs, fd, s_f.at[2], r_f.at[1], d, 2 * z + 1)
    d_self = pltpu.make_async_copy(fs, fd, s_loc.at[4])

    @pl.when(c == 0)
    def _():
        u_copy.start()
        up_ref[...] = fs[...]

    @pl.when(c == 1)
    def _():
        d0_copy.start()

        @pl.when(s == d)
        def _():
            d_self.start()
            d_self.wait()

        @pl.when(s != d)
        def _():
            d1_copy.start()

        u_copy.wait_recv()
        up_ref[...] = fu[...]

    @pl.when(jnp.logical_not(own_final))
    def _():
        d0_copy.wait_recv()

    down_ref[...] = fd[...]

    @pl.when(c == 0)
    def _():
        u_copy.wait_send()
        for k in range(1, NY):
            wy_copy(k).wait_send()
        for k in range(1, NX):
            ux_copy(k).wait_send()
        for k in range(NX):
            ul_copy(k).wait_send()

    @pl.when(c == 1)
    def _():
        d0_copy.wait_send()

        @pl.when(s != d)
        def _():
            d1_copy.wait_send()

        for k in range(1, NX):
            dx_copy(k).wait_send()
        for k in range(NX):
            dl_copy(k).wait_send()

    c_copy.wait_send()
    for k in range(1, NS):
        row_copy(k).wait_send()
        id_copy(k).wait_send()
        g1_copy(k).wait_send()
    for k in range(1, ND):
        gain_copy(k).wait_send()
        g2_copy(k).wait_send()
    for k in range(1, NY):
        na_copy(k).wait_send()
        ga_copy(k).wait_send()
        dn_copy(k).wait_send()
    for k in range(1, NX):
        x_copy(k).wait_send()
    for k in range(1, NZ):
        z_copy(k).wait_send()


def exchange(rows, ids, w_up, w_down, unit, gain_placed):
    vm = pl.BlockSpec(memory_space=pltpu.VMEM)
    hbm = pl.BlockSpec(memory_space=pl.ANY)
    sem = pltpu.SemaphoreType.DMA
    pairs = [NS, NS, ND, NY, NX, NX, NY, NY, NY, 1, NX, NZ, 3, NS, ND]
    sems = [sem((5,))]
    for n in pairs:
        sems += [sem((n,)), sem((n,))]
    return pl.pallas_call(
        kernel,
        out_shape=(
            jax.ShapeDtypeStruct((TOK, D), F32),
            jax.ShapeDtypeStruct((TOK, D), BF),
            jax.ShapeDtypeStruct((1, D), F32),
            jax.ShapeDtypeStruct((1, D), F32),
            jax.ShapeDtypeStruct((FF_DP, WIN), BF),
            jax.ShapeDtypeStruct((FF_DP, WIN), BF),
        ),
        in_specs=[hbm, hbm, hbm, hbm, vm, vm],
        out_specs=(vm,) * 6,
        scratch_shapes=[
            pltpu.VMEM((NS, CAP, D), BF),
            pltpu.VMEM((NS, 1, 128), jnp.int32),
            pltpu.VMEM((ND, 1, D), F32),
            pltpu.VMEM((NY, NX, ROWS_DP, FQ), BF),
            pltpu.VMEM((NX, FF_DP, D), BF),
            pltpu.VMEM((2, NY, TOK, D), BF),
            pltpu.VMEM((2, NY * TOK, FQ), BF),
            pltpu.VMEM((NY * TOK, FQ), F32),
            pltpu.VMEM((NY, TOK, D), BF),
            pltpu.VMEM((NY, TOK, D), BF),
            pltpu.VMEM((2, FQ, D), BF),
            pltpu.VMEM((FQ, D), BF),
            pltpu.VMEM((FQ, D), BF),
            pltpu.VMEM((NX, FF_DP, D), BF),
            pltpu.VMEM((FF_DP, D), BF),
            pltpu.VMEM((NZ, FF_DP, WIN), BF),
            pltpu.VMEM((FF_DP, WIN), BF),
            pltpu.VMEM((FF_DP, WIN), BF),
            pltpu.VMEM((FF_DP, WIN), BF),
            pltpu.VMEM((1, D), F32),
            pltpu.VMEM((NS, 1, D), F32),
            pltpu.VMEM((1, D), F32),
            pltpu.VMEM((ND, 1, D), F32),
            *sems,
        ],
        compiler_params=pltpu.CompilerParams(
            collective_id=0, has_side_effects=True, vmem_limit_bytes=56 * 2**20
        ),
    )(rows, ids, w_up, w_down, unit, gain_placed)


def per_device(
    queries,
    key_rows,
    value_rows,
    resid_in,
    llm_grad,
    vision_slot,
    window_mask,
    w_up,
    w_down,
    norm_gain,
):
    s_at = lax.axis_index("seq")
    d_at = lax.axis_index("dp")
    query = queries[0]
    tokens, feat_dim = query.shape
    att_scale = 1.0 / math.sqrt(HDIM)

    slot_ids = vision_slot[0]
    n_pos = slot_ids.shape[0]
    owner = jnp.where(slot_ids >= 0, slot_ids // tokens, NS)
    before = jnp.arange(n_pos)[None, :] < jnp.arange(n_pos)[:, None]
    rank = jnp.sum(((owner[:, None] == owner[None, :]) & before).astype(jnp.int32), axis=1)
    target = jnp.where(slot_ids >= 0, owner * CAP + rank, -1)
    hit = jnp.arange(NS * CAP)[:, None] == target[None, :]
    send_rows = jnp.dot(hit.astype(BF), llm_grad[0], preferred_element_type=F32).astype(BF)
    landing = jnp.max(jnp.where(hit, (slot_ids % tokens)[None, :], -1), axis=1)
    lane = jnp.arange(128)
    send_ids = jnp.where(
        (lane // CAP == s_at % 4)[None, :], jnp.tile(landing.reshape(NS, CAP), (1, 4)), -1
    )

    allowed = jnp.repeat(jnp.repeat(window_mask[0] > 0, BLK, axis=0), BLK, axis=1)
    q_heads = query.reshape(tokens, HEADS, HDIM)
    k_heads = key_rows[0].reshape(tokens, HEADS, HDIM)
    v_heads = value_rows[0].reshape(tokens, HEADS, HDIM)
    scores = jnp.einsum("qhd,khd->hqk", q_heads, k_heads, preferred_element_type=F32) * att_scale
    masked = jnp.where(allowed[None], scores, -jnp.inf)
    highest = jnp.max(masked, axis=2, keepdims=True)
    exp_terms = jnp.where(allowed[None], jnp.exp(masked - highest), 0.0)
    attn_probs = exp_terms / jnp.sum(exp_terms, axis=2, keepdims=True)
    probs_low = attn_probs.astype(BF)
    attn_heads = jnp.einsum(
        "hqk,khd->qhd", probs_low, v_heads, preferred_element_type=F32
    ).astype(BF)
    attn_out = attn_heads.reshape(tokens, feat_dim)
    hidden = resid_in[0].astype(F32) + attn_out.astype(F32)
    center = jnp.mean(hidden, axis=1, keepdims=True)
    variance = jnp.mean(jnp.square(hidden - center), axis=1, keepdims=True)
    inverse = lax.rsqrt(variance + 1e-06)
    normal_unit = (hidden - center) * inverse

    mine = (jnp.arange(feat_dim) // ROWS_DP) == d_at
    gain_placed = jnp.where(mine, jnp.tile(norm_gain.astype(F32), ND), 0.0)[None, :]

    d_normed, grad_rows, gain_wide, grad_gain, up_win, down_win = exchange(
        send_rows.reshape(NS, CAP, feat_dim),
        send_ids.reshape(NS, 1, 128),
        w_up,
        w_down,
        normal_unit,
        gain_placed,
    )

    d_unit = d_normed * gain_wide
    d_hidden = inverse * (
        d_unit
        - jnp.mean(d_unit, axis=1, keepdims=True)
        - normal_unit * jnp.mean(d_unit * normal_unit, axis=1, keepdims=True)
    )
    grad_resid = (grad_rows.astype(F32) + d_hidden).astype(BF)
    grad_heads = grad_resid.reshape(tokens, HEADS, HDIM)
    grad_value = jnp.einsum(
        "hqk,qhd->khd", probs_low, grad_heads, preferred_element_type=F32
    ).astype(BF)
    d_probs = jnp.einsum("qhd,khd->hqk", grad_heads, v_heads, preferred_element_type=F32)
    delta = jnp.einsum("qhd,qhd->hq", grad_heads, attn_heads, preferred_element_type=F32)
    d_scores = (attn_probs * (d_probs - delta[:, :, None]) * att_scale).astype(BF)
    grad_query = jnp.einsum("hqk,khd->qhd", d_scores, k_heads, preferred_element_type=F32).astype(BF)
    grad_key = jnp.einsum("hqk,qhd->khd", d_scores, q_heads, preferred_element_type=F32).astype(BF)

    z_at = s_at // 2
    up_own = lax.dynamic_slice_in_dim(
        up_win, 32 * (z_at % 4) + ROWS_DP * (s_at % 2), ROWS_DP, axis=1
    ).T
    down_own = lax.dynamic_slice_in_dim(
        down_win, 32 * ((d_at // 2) % 4) + ROWS_DP * (d_at % 2), ROWS_DP, axis=1
    )
    return (
        grad_query.reshape(1, tokens, feat_dim),
        grad_key.reshape(1, tokens, feat_dim),
        grad_value.reshape(1, tokens, feat_dim),
        grad_resid[None],
        up_own,
        down_own,
        grad_gain.reshape(feat_dim),
    )


def solution(mesh):
    row3 = P("dp", "seq", None)
    in_specs = (
        row3,
        row3,
        row3,
        row3,
        row3,
        P("dp", "seq"),
        row3,
        P("dp", None),
        P("dp", None),
        P("dp"),
    )
    out_specs = (row3, row3, row3, row3, P("seq", "dp"), P("seq", "dp"), P())
    return jax.shard_map(
        per_device, mesh=mesh, in_specs=in_specs, out_specs=out_specs, check_vma=False
    )
```

```python
import math

import jax
import jax.numpy as jnp
from jax import lax
from jax.experimental import pallas as pl
from jax.experimental.pallas import tpu as pltpu
from jax.sharding import PartitionSpec as P

HEADS = 16
HDIM = 80
BLK = 64
D = 1280
FF = 2560
TOK = 128
POS = 192
NS = 16
ND = 16
CAP = 32
NY, NX, NZ = 4, 4, 8
FQ = FF // NY
ROWS_DP = D // ND
FF_DP = FF // ND
WIN = 256
NP = 5
PW = D // NP
NR = 5
RW = FF_DP // NR
MESH = pl.DeviceIdType.MESH
BF = jnp.bfloat16
F32 = jnp.float32


def mm(left, right, left_dim, right_dim):
    return lax.dot_general(
        left, right, (((left_dim,), (right_dim,)), ((), ())), preferred_element_type=F32
    )


def iota(shape, dim):
    return lax.broadcasted_iota(jnp.int32, shape, dim)


def to_column(row):
    n = row.shape[1]
    same = iota((n, n), 0) == iota((n, n), 1)
    return jnp.sum(jnp.where(same, row, 0.0), axis=1, keepdims=True)


def window_start(z):
    return pl.multiple_of(128 * ((5 * z) // 4), 128)


SEMS = {
    "gr": ND, "rr": NP * NS, "ri": NS, "wy": NY, "wx": NX, "rl": NX, "na": NY, "ga": NP * NY,
    "dn": NY, "c": 5, "x": NR * NX, "z": NR * NZ, "f": 3, "g1": NS, "g2": ND,
}


def kernel(
    q_ref, k_ref, v_ref, resid_ref, llm_ref, slot_ref, mask_ref, wup_ref, wdown_ref, ngain_ref,
    gq_ref, gk_ref, gv_ref, gresid_ref, up_ref, down_ref, ggain_ref,
    rs, rr, ids, ri, gsh, gr, wu, wd, ra, la, gate, dact, dns, dnr, gt, cr, xs, xr, zs, zr,
    fs, fu, fd, gp, gs1, gp2, gs2, probs, att, unit, inv, s_loc, *sems,
):
    names = list(SEMS)
    send = {n: sems[2 * i] for i, n in enumerate(names)}
    recv = {n: sems[2 * i + 1] for i, n in enumerate(names)}
    s = lax.axis_index("seq")
    d = lax.axis_index("dp")
    z, c = s // 2, s % 2
    y, x = d // NX, d % NX
    scale = 1.0 / math.sqrt(HDIM)

    def remote(src, dst, name, at, to_s, to_d, at_recv=None):
        return pltpu.make_async_remote_copy(
            src_ref=src,
            dst_ref=dst,
            send_sem=send[name].at[at],
            recv_sem=recv[name].at[at if at_recv is None else at_recv],
            device_id=(to_s, to_d),
            device_id_type=MESH,
        )

    def y_peer(k):
        return ((y + k) % NY) * NX + x

    def x_peer(k):
        return y * NX + (x + k) % NX

    barrier = pltpu.get_barrier_semaphore()
    for k in range(1, NS):
        pl.semaphore_signal(barrier, inc=1, device_id=((s + k) % NS, d), device_id_type=MESH)
    for k in range(1, ND):
        pl.semaphore_signal(barrier, inc=1, device_id=(s, (d + k) % ND), device_id_type=MESH)
    from_s = 2 * (d // 2) + 1
    own_final = jnp.logical_and(from_s == s, s == d)

    @pl.when(jnp.logical_not(own_final))
    def _():
        pl.semaphore_signal(barrier, inc=1, device_id=(from_s, s), device_id_type=MESH)

    slot_row = slot_ref[...].astype(F32)
    slot_col = to_column(slot_row)
    owner_row = jnp.floor(slot_row * (1.0 / TOK))
    owner_col = jnp.floor(slot_col * (1.0 / TOK))
    at0, at1 = iota((POS, POS), 0), iota((POS, POS), 1)
    same = owner_col == owner_row
    rank_row = jnp.sum(jnp.where(same & (at0 < at1), 1.0, 0.0), axis=0, keepdims=True)
    rank_col = jnp.sum(jnp.where(same & (at1 < at0), 1.0, 0.0), axis=1, keepdims=True)
    target_row = jnp.where(slot_row >= 0.0, owner_row * CAP + rank_row, -1.0)
    target_col = jnp.where(slot_col >= 0.0, owner_col * CAP + rank_col, -1.0)
    hit = iota((NS * CAP, POS), 0).astype(F32) == target_row
    pick = jnp.where(hit, 1.0, 0.0).astype(BF)
    for p in range(NP):
        rs[p] = mm(pick, llm_ref[:, PW * p : PW * p + PW], 1, 0).astype(BF).reshape(NS, CAP, PW)
    lane = iota((1, 128), 1)
    lane_slot = (lane % CAP).astype(F32)
    mine = lane // CAP == s % 4
    landing = slot_col - owner_col * TOK + 1.0
    for o in range(NS):
        found = jnp.where((target_col == lane_slot + float(o * CAP)) & mine, landing, 0.0)
        ids[o] = jnp.sum(found, axis=0, keepdims=True) - 1.0
    ngain_col = to_column(ngain_ref[...].astype(F32))
    place_gain = iota((ROWS_DP, D), 1) == iota((ROWS_DP, D), 0) + d * ROWS_DP
    gsh[...] = jnp.sum(jnp.where(place_gain, ngain_col, 0.0), axis=0, keepdims=True)

    pl.semaphore_wait(barrier, NS + ND - 2 + 2 * c - jnp.where(own_final, 1, 0))

    def gain_copy(k):
        return remote(gsh, gr.at[d], "gr", k, s, (d + k) % ND)

    def row_copy(p, k):
        to = (s + k) % NS
        return remote(rs.at[p, to], rr.at[p, s], "rr", p * NS + k, to, d)

    def id_copy(k):
        to = (s + k) % NS
        return remote(ids.at[to], ri.at[s], "ri", k, to, d)

    far_first = (8, 7, 9, 6, 10, 5, 11, 4, 12, 3, 13, 2, 14, 1, 15)
    for k in far_first:
        id_copy(k).start()
    for k in far_first:
        row_copy(0, k).start()
    for k in range(1, ND):
        gain_copy(k).start()

    def quarter(q):
        return wup_ref.at[:, pl.ds(pl.multiple_of(q * FQ, 128), FQ)]

    def wy_copy(k):
        return remote(quarter((y + k) % NY), wu.at[y, x], "wy", k, s, y_peer(k))

    def ux_copy(k):
        return remote(wu.at[:, x], wu.at[:, x], "wx", k, s, x_peer(k))

    def dx_copy(k):
        return remote(wd.at[x], wd.at[x], "wx", k, s, x_peer(k))

    def ul_copy(k):
        at = (x + NX - k) % NX
        return remote(wu.at[:, at], wu.at[:, at], "rl", k, s + 1, d)

    def dl_copy(k):
        at = (x + NX - k) % NX
        return remote(wd.at[at], wd.at[at], "rl", k, s - 1, d)

    own_up = pltpu.make_async_copy(quarter(y), wu.at[y, x], s_loc.at[0])
    own_down = pltpu.make_async_copy(wdown_ref, wd.at[x], s_loc.at[1])

    @pl.when(c == 0)
    def _():
        for k in (2, 1, 3):
            wy_copy(k).start()
        own_up.start()
        own_up.wait()

    @pl.when(c == 1)
    def _():
        own_down.start()
        own_down.wait()
        for k in (2, 1, 3):
            dx_copy(k).start()
        dl_copy(0).start()

    for p in range(1, NP):
        for k in far_first:
            row_copy(p, k).start()
    for p in range(NP):
        rr[p, s] = rs[p, s]
    ri[s] = ids[s]

    row_late = iota((TOK, TOK), 0) >= BLK
    col_late = iota((TOK, TOK), 1) >= BLK
    flags = [[mask_ref[0, i : i + 1, j : j + 1] for j in range(2)] for i in range(2)]
    allowed = (
        jnp.where(
            row_late,
            jnp.where(col_late, flags[1][1], flags[1][0]),
            jnp.where(col_late, flags[0][1], flags[0][0]),
        )
        > 0
    )

    def attend(h):
        at = slice(HDIM * h, HDIM * h + HDIM)
        scores = mm(q_ref[:, at], k_ref[:, at], 1, 1) * scale
        masked = jnp.where(allowed, scores, -jnp.inf)
        highest = jnp.max(masked, axis=1, keepdims=True)
        terms = jnp.where(allowed, jnp.exp(masked - highest), 0.0)
        prob = terms * (1.0 / jnp.sum(terms, axis=1, keepdims=True))
        probs[h] = prob
        att[:, at] = mm(prob.astype(BF), v_ref[:, at], 1, 0).astype(BF)

    for h in range(HEADS // 2):
        attend(h)

    @pl.when(c == 0)
    def _():
        for k in range(1, NY):
            wy_copy(k).wait_recv()
        for k in (2, 1, 3):
            ux_copy(k).start()
        ul_copy(0).start()

    for h in range(HEADS // 2, HEADS):
        attend(h)

    gr[d] = gsh[...]
    for k in range(1, ND):
        gain_copy(k).wait_recv()
    gain_full = jnp.sum(gr[...], axis=0)

    def unit_step(i, carry):
        rows = pl.ds(pl.multiple_of(i * 32, 32), 32)
        hidden = resid_ref[rows, :].astype(F32) + att[rows, :].astype(F32)
        center = jnp.mean(hidden, axis=1, keepdims=True)
        away = hidden - center
        inverse = lax.rsqrt(jnp.mean(away * away, axis=1, keepdims=True) + 1e-06)
        inv[rows, :] = inverse
        out = away * inverse
        unit[rows, :] = out
        ra[0, y, rows, :] = (out * gain_full).astype(BF)
        return carry

    lax.fori_loop(0, TOK // 32, unit_step, 0)

    def na_copy(k):
        return remote(ra.at[0, y], ra.at[0, y], "na", k, s, y_peer(k))

    for k in (2, 1, 3):
        na_copy(k).start()

    @pl.when(c == 1)
    def _():
        for k in (1, 3, 2):
            dx_copy(k).wait_recv()
            dl_copy(k).start()

    for k in range(1, NS):
        id_copy(k).wait_recv()
    token = iota((TOK, 128), 0).astype(F32)
    place = jnp.concatenate(
        [
            jnp.where(token == jnp.max(ri[4 * j : 4 * j + 4], axis=0), 1.0, 0.0).astype(BF)
            for j in range(4)
        ],
        axis=1,
    )

    def piece(p):
        return slice(PW * p, PW * p + PW)

    def ga_copy(p, k):
        view = ra.at[1, y, :, piece(p)]
        return remote(view, view, "ga", p * NY + k, s, y_peer(k))

    def rows_in(p):
        for k in range(1, NS):
            row_copy(p, k).wait_recv()
        ra[1, y, :, piece(p)] = mm(place, rr[p].reshape(NS * CAP, PW), 1, 0).astype(BF)
        for k in (2, 1, 3):
            ga_copy(p, k).start()

    rows_in(0)
    rows_in(1)
    rows_in(2)

    @pl.when(c == 0)
    def _():
        for k in (1, 3, 2):
            ux_copy(k).wait_recv()
            ul_copy(k).start()

    @pl.when(c == 1)
    def _():
        for k in range(NX):
            ul_copy(k).wait_recv()

    for k in range(1, NY):
        na_copy(k).wait_recv()
    half = 2 * TOK

    def up_step(i, carry):
        rows = pl.ds(pl.multiple_of(i * half, half), half)
        pre = mm(ra[0, pl.ds(2 * i, 2)].reshape(half, D), wu[...].reshape(D, FQ), 1, 0)
        sig = jax.nn.sigmoid(1.702 * pre)
        la[1, rows, :] = (pre * sig).astype(BF)
        gate[rows, :] = sig + 1.702 * pre * sig * (1.0 - sig)
        return carry

    lax.fori_loop(0, 2, up_step, 0)

    rows_in(3)
    rows_in(4)

    @pl.when(c == 0)
    def _():
        for k in range(NX):
            dl_copy(k).wait_recv()

    def cd_copy(p):
        return remote(gt.at[1, :, piece(p)], cr.at[:, piece(p)], "c", p, s + 1, d)

    def cu_copy(i):
        rows = slice(128 * i, 128 * i + 128)
        return remote(gt.at[0, rows], cr.at[rows], "c", i, s - 1, d)

    def down_in(p):
        cd_copy(p).wait_recv()
        xs[:, piece(p)] = (
            gt[1, :, piece(p)].astype(F32) + cr[:, piece(p)].astype(F32)
        ).astype(BF)

    for p in range(NP):
        for k in range(1, NY):
            ga_copy(p, k).wait_recv()
        grads = ra[1, :, :, piece(p)].reshape(NY * TOK, PW)
        part = mm(grads, wd[:, :, piece(p)].reshape(FQ, PW), 1, 1)
        dact[...] = part if p == 0 else dact[...] + part
        gt[1, :, piece(p)] = mm(la[1], grads, 0, 0).astype(BF)

        @pl.when(c == 0)
        def _(p=p):
            cd_copy(p).start()

        if p > 0:

            @pl.when(c == 1)
            def _(p=p):
                down_in(p - 1)

    la[0] = (dact[...] * gate[...]).astype(BF)

    def x_copy(r, k):
        to = (x + k) % NX
        rows = pl.ds(pl.multiple_of(to * FF_DP + r * RW, RW), RW)
        return remote(
            xs.at[rows], xr.at[x, pl.ds(r * RW, RW)], "x", r * NX + k, s, y * NX + to
        )

    @pl.when(c == 1)
    def _():
        down_in(NP - 1)
        for r in range(NR):
            for k in (2, 1, 3):
                x_copy(r, k).start()

    for i in range(FQ // 128):
        rows = slice(128 * i, 128 * i + 128)
        gt[0, rows, :] = mm(la[0, :, rows], ra[0].reshape(NY * TOK, D), 0, 0).astype(BF)

        @pl.when(c == 1)
        def _(i=i):
            cu_copy(i).start()

    def norm_step(i, acc):
        rows = pl.ds(pl.multiple_of(i * half, half), half)
        part = mm(la[0, rows, :], wu[...].reshape(D, FQ), 1, 1)
        dns[pl.ds(2 * i, 2)] = part.astype(BF).reshape(2, TOK, D)
        normed = ra[0, pl.ds(2 * i, 2)].reshape(half, D).astype(F32)
        return acc + jnp.sum(part * normed, axis=0, keepdims=True)

    gp[...] = lax.fori_loop(0, 2, norm_step, jnp.zeros((1, D), F32))

    def dn_copy(k):
        to = (y + k) % NY
        return remote(dns.at[to], dnr.at[y], "dn", k, s, to * NX + x)

    for k in (2, 1, 3):
        dn_copy(k).start()

    def g1_copy(k):
        return remote(gp, gs1.at[s], "g1", k, (s + k) % NS, d)

    for k in range(1, NS):
        g1_copy(k).start()

    @pl.when(c == 0)
    def _():
        for i in range(FQ // 128):
            cu_copy(i).wait_recv()
        for r in range(NR):
            for b in range(NX):
                rows = pl.ds(b * FF_DP + r * RW, RW)
                xs[rows, :] = (gt[0, rows, :].astype(F32) + cr[rows, :].astype(F32)).astype(BF)
            for k in (2, 1, 3):
                x_copy(r, k).start()

    def z_copy(r, k):
        to = (z + k) % NZ
        rows = pl.ds(r * RW, RW)
        return remote(
            zs.at[rows, pl.ds(window_start(to), WIN)],
            zr.at[z, rows],
            "z",
            r * NZ + k,
            2 * to + c,
            d,
        )

    for r in range(NR):
        rows = pl.ds(r * RW, RW)
        own = pl.ds(pl.multiple_of(x * FF_DP + r * RW, RW), RW)
        for k in range(1, NX):
            x_copy(r, k).wait_recv()
        xr[x, rows] = xs[own, :]
        zs[rows, :] = jnp.sum(xr[:, rows, :].astype(F32), axis=0).astype(BF)
        for k in (4, 3, 5, 2, 6, 1, 7):
            z_copy(r, k).start()
        zr[z, rows] = zs[rows, pl.ds(window_start(z), WIN)]

    gs1[s] = gp[...]
    for k in range(1, NS):
        g1_copy(k).wait_recv()
    gp2[...] = jnp.sum(gs1[...], axis=0)

    def g2_copy(k):
        return remote(gp2, gs2.at[d], "g2", k, s, (d + k) % ND)

    for k in range(1, ND):
        g2_copy(k).start()

    dnr[y] = dns[y]
    for k in range(1, NY):
        dn_copy(k).wait_recv()
    gain_again = jnp.sum(gr[...], axis=0)

    def resid_step(i, carry):
        rows = pl.ds(pl.multiple_of(i * 32, 32), 32)
        d_unit = jnp.sum(dnr[:, rows, :].astype(F32), axis=0) * gain_again
        normal = unit[rows, :]
        first = jnp.mean(d_unit, axis=1, keepdims=True)
        second = jnp.mean(d_unit * normal, axis=1, keepdims=True)
        d_hidden = inv[rows, :] * (d_unit - first - normal * second)
        gresid_ref[rows, :] = (ra[1, y, rows, :].astype(F32) + d_hidden).astype(BF)
        return carry

    lax.fori_loop(0, TOK // 32, resid_step, 0)

    for h in range(HEADS):
        at = slice(HDIM * h, HDIM * h + HDIM)
        grad = gresid_ref[:, at]
        prob = probs[h]
        gv_ref[:, at] = mm(prob.astype(BF), grad, 0, 0).astype(BF)
        d_probs = mm(grad, v_ref[:, at], 1, 1)
        delta = jnp.sum(
            grad.astype(F32) * att[:, at].astype(F32), axis=1, keepdims=True
        )
        d_scores = (prob * (d_probs - delta) * scale).astype(BF)
        gq_ref[:, at] = mm(d_scores, k_ref[:, at], 1, 0).astype(BF)
        gk_ref[:, at] = mm(d_scores, q_ref[:, at], 0, 0).astype(BF)

    factor = 1.0 / math.sqrt(NS * ND * TOK)
    gs2[d] = gp2[...]
    for k in range(1, ND):
        g2_copy(k).wait_recv()
    ggain_ref[...] = jnp.sum(gs2[...], axis=0) * factor / gain_again

    for r in range(NR):
        for k in range(1, NZ):
            z_copy(r, k).wait_recv()
    fs[...] = (jnp.sum(zr[...].astype(F32), axis=0) * factor).astype(BF)

    u_copy = remote(fs, fu, "f", 0, s + 1, d)
    d0_copy = remote(fs, fd, "f", 1, d, 2 * z)
    d1_copy = remote(fs, fd, "f", 2, d, 2 * z + 1, 1)
    own_down_out = pltpu.make_async_copy(fs, fd, s_loc.at[2])

    def chosen(first):
        return jnp.where(
            iota((ROWS_DP, WIN), 1) == iota((ROWS_DP, WIN), 0) + first, 1.0, 0.0
        ).astype(BF)

    own_lanes = chosen(32 * (z % 4) + ROWS_DP * c)

    @pl.when(c == 0)
    def _():
        u_copy.start()
        up_ref[...] = mm(own_lanes, fs[...], 1, 1).astype(BF)

    @pl.when(c == 1)
    def _():
        d0_copy.start()

        @pl.when(s == d)
        def _():
            own_down_out.start()
            own_down_out.wait()

        @pl.when(s != d)
        def _():
            d1_copy.start()

        u_copy.wait_recv()
        up_ref[...] = mm(own_lanes, fu[...], 1, 1).astype(BF)

    @pl.when(jnp.logical_not(own_final))
    def _():
        d0_copy.wait_recv()

    down_ref[...] = mm(
        fd[...], chosen(32 * ((d // 2) % 4) + ROWS_DP * (d % 2)), 1, 1
    ).astype(BF)

    @pl.when(c == 0)
    def _():
        u_copy.wait_send()
        for k in range(1, NY):
            wy_copy(k).wait_send()
        for k in range(1, NX):
            ux_copy(k).wait_send()
        for k in range(NX):
            ul_copy(k).wait_send()
        for p in range(NP):
            cd_copy(p).wait_send()

    @pl.when(c == 1)
    def _():
        d0_copy.wait_send()

        @pl.when(s != d)
        def _():
            d1_copy.wait_send()

        for k in range(1, NX):
            dx_copy(k).wait_send()
        for k in range(NX):
            dl_copy(k).wait_send()
        for i in range(FQ // 128):
            cu_copy(i).wait_send()

    for k in range(1, NS):
        for p in range(NP):
            row_copy(p, k).wait_send()
        id_copy(k).wait_send()
        g1_copy(k).wait_send()
    for k in range(1, ND):
        gain_copy(k).wait_send()
        g2_copy(k).wait_send()
    for k in range(1, NY):
        na_copy(k).wait_send()
        for p in range(NP):
            ga_copy(p, k).wait_send()
        dn_copy(k).wait_send()
    for r in range(NR):
        for k in range(1, NX):
            x_copy(r, k).wait_send()
        for k in range(1, NZ):
            z_copy(r, k).wait_send()


def layer(*args):
    vm = pl.BlockSpec(memory_space=pltpu.VMEM)
    hbm = pl.BlockSpec(memory_space=pl.ANY)
    sem = pltpu.SemaphoreType.DMA
    sems = [sem((4,))]
    for n in SEMS.values():
        sems += [sem((n,)), sem((n,))]
    out = jax.ShapeDtypeStruct
    return pl.pallas_call(
        kernel,
        out_shape=(
            out((TOK, D), BF),
            out((TOK, D), BF),
            out((TOK, D), BF),
            out((TOK, D), BF),
            out((ROWS_DP, FF_DP), BF),
            out((FF_DP, ROWS_DP), BF),
            out((1, D), F32),
        ),
        in_specs=[vm] * 7 + [hbm, hbm, vm],
        out_specs=(vm,) * 7,
        scratch_shapes=[
            pltpu.VMEM((NP, NS, CAP, PW), BF),
            pltpu.VMEM((NP, NS, CAP, PW), BF),
            pltpu.VMEM((NS, 1, 128), F32),
            pltpu.VMEM((NS, 1, 128), F32),
            pltpu.VMEM((1, D), F32),
            pltpu.VMEM((ND, 1, D), F32),
            pltpu.VMEM((NY, NX, ROWS_DP, FQ), BF),
            pltpu.VMEM((NX, FF_DP, D), BF),
            pltpu.VMEM((2, NY, TOK, D), BF),
            pltpu.VMEM((2, NY * TOK, FQ), BF),
            pltpu.VMEM((NY * TOK, FQ), F32),
            pltpu.VMEM((NY * TOK, FQ), F32),
            pltpu.VMEM((NY, TOK, D), BF),
            pltpu.VMEM((NY, TOK, D), BF),
            pltpu.VMEM((2, FQ, D), BF),
            pltpu.VMEM((FQ, D), BF),
            pltpu.VMEM((FQ, D), BF),
            pltpu.VMEM((NX, FF_DP, D), BF),
            pltpu.VMEM((FF_DP, D), BF),
            pltpu.VMEM((NZ, FF_DP, WIN), BF),
            pltpu.VMEM((FF_DP, WIN), BF),
            pltpu.VMEM((FF_DP, WIN), BF),
            pltpu.VMEM((FF_DP, WIN), BF),
            pltpu.VMEM((1, D), F32),
            pltpu.VMEM((NS, 1, D), F32),
            pltpu.VMEM((1, D), F32),
            pltpu.VMEM((ND, 1, D), F32),
            pltpu.VMEM((HEADS, TOK, TOK), F32),
            pltpu.VMEM((TOK, D), BF),
            pltpu.VMEM((TOK, D), F32),
            pltpu.VMEM((TOK, 1), F32),
            *sems,
        ],
        compiler_params=pltpu.CompilerParams(
            collective_id=0, has_side_effects=True, vmem_limit_bytes=56 * 2**20
        ),
    )(*args)


def per_device(
    queries, key_rows, value_rows, resid_in, llm_grad, vision_slot, window_mask, w_up, w_down,
    norm_gain,
):
    grad_query, grad_key, grad_value, grad_resid, grad_up, grad_down, grad_gain = layer(
        queries[0],
        key_rows[0],
        value_rows[0],
        resid_in[0],
        llm_grad[0],
        vision_slot,
        window_mask,
        w_up,
        w_down,
        norm_gain.reshape(1, ROWS_DP),
    )
    return (
        grad_query[None],
        grad_key[None],
        grad_value[None],
        grad_resid[None],
        grad_up,
        grad_down,
        grad_gain.reshape(D),
    )


def solution(mesh):
    row3 = P("dp", "seq", None)
    in_specs = (
        row3,
        row3,
        row3,
        row3,
        row3,
        P("dp", "seq"),
        row3,
        P("dp", None),
        P("dp", None),
        P("dp"),
    )
    out_specs = (row3, row3, row3, row3, P("seq", "dp"), P("seq", "dp"), P())
    return jax.shard_map(
        per_device, mesh=mesh, in_specs=in_specs, out_specs=out_specs, check_vma=False
    )
```

```python
import math

import jax
import jax.numpy as jnp
from jax import lax
from jax.experimental import pallas as pl
from jax.experimental.pallas import tpu as pltpu
from jax.sharding import PartitionSpec as P

HEADS = 16
HDIM = 80
BLK = 64
D = 1280
FF = 2560
TOK = 128
POS = 192
NS = 16
ND = 16
CAP = 32
NY, NX, NZ = 4, 4, 8
FQ = FF // NY
ROWS_DP = D // ND
FF_DP = FF // ND
WIN = 256
NP = 5
PW = D // NP
NR = 5
RW = FF_DP // NR
MESH = pl.DeviceIdType.MESH
BF = jnp.bfloat16
F32 = jnp.float32


def mm(left, right, left_dim, right_dim):
    return lax.dot_general(
        left, right, (((left_dim,), (right_dim,)), ((), ())), preferred_element_type=F32
    )


def iota(shape, dim):
    return lax.broadcasted_iota(jnp.int32, shape, dim)


def to_column(row):
    n = row.shape[1]
    same = iota((n, n), 0) == iota((n, n), 1)
    return jnp.sum(jnp.where(same, row, 0.0), axis=1, keepdims=True)


def window_start(z):
    return pl.multiple_of(128 * ((5 * z) // 4), 128)


SEMS = {
    "gr": ND, "rr": NP * NS, "ri": NS, "wy": NY, "wx": NX, "rl": NX, "na": NY, "nf": 2, "ga": NP * NY, "gf": NP * 2,
    "dn": NY, "c": 5, "x": NR * NX, "z": NR * NZ, "f": 3, "g1": NS, "g2": ND,
}


def kernel(
    q_hbm, k_hbm, v_hbm, resid_hbm, llm_hbm, slot_ref, mask_ref, wup_ref, wdown_ref, ngain_ref,
    gq_hbm, gk_hbm, gv_hbm, gresid_hbm, up_ref, down_ref, ggain_ref,
    q_ref, k_ref, v_ref, resid_ref, llm_ref, gq_ref, gk_ref, gv_ref, gresid_ref,
    rs, rr, ids, ri, gsh, gr, wu, wd, ra, la, gate, dact, dns, dnr, gt, cr, xs, xr, zs, zr,
    fs, fu, fd, gp, gs1, gp2, gs2, probs, att, unit, inv, s_loc, *sems,
):
    names = list(SEMS)
    send = {n: sems[2 * i] for i, n in enumerate(names)}
    recv = {n: sems[2 * i + 1] for i, n in enumerate(names)}
    s = lax.axis_index("seq")
    d = lax.axis_index("dp")
    z, c = s // 2, s % 2
    y, x = d // NX, d % NX
    scale = 1.0 / math.sqrt(HDIM)

    def remote(src, dst, name, at, to_s, to_d, at_recv=None):
        return pltpu.make_async_remote_copy(
            src_ref=src,
            dst_ref=dst,
            send_sem=send[name].at[at],
            recv_sem=recv[name].at[at if at_recv is None else at_recv],
            device_id=(to_s, to_d),
            device_id_type=MESH,
        )

    def y_peer(k):
        return ((y + k) % NY) * NX + x

    def x_peer(k):
        return y * NX + (x + k) % NX

    def local(src, dst, at):
        return pltpu.make_async_copy(src, dst, s_loc.at[at])

    loads = [
        local(llm_hbm, llm_ref, 3),
        local(q_hbm, q_ref, 4),
        local(k_hbm, k_ref, 5),
        local(v_hbm, v_ref, 6),
        local(resid_hbm, resid_ref, 7),
    ]
    stores = [
        local(gresid_ref, gresid_hbm, 8),
        local(gq_ref, gq_hbm, 9),
        local(gk_ref, gk_hbm, 10),
        local(gv_ref, gv_hbm, 11),
    ]
    for copy in loads:
        copy.start()

    barrier = pltpu.get_barrier_semaphore()
    for k in range(1, NS):
        pl.semaphore_signal(barrier, inc=1, device_id=((s + k) % NS, d), device_id_type=MESH)
    for k in range(1, ND):
        pl.semaphore_signal(barrier, inc=1, device_id=(s, (d + k) % ND), device_id_type=MESH)
    from_s = 2 * (d // 2) + 1
    own_final = jnp.logical_and(from_s == s, s == d)

    @pl.when(jnp.logical_not(own_final))
    def _():
        pl.semaphore_signal(barrier, inc=1, device_id=(from_s, s), device_id_type=MESH)

    slot_row = slot_ref[...].astype(F32)
    slot_col = to_column(slot_row)
    owner_row = jnp.floor(slot_row * (1.0 / TOK))
    owner_col = jnp.floor(slot_col * (1.0 / TOK))
    at0, at1 = iota((POS, POS), 0), iota((POS, POS), 1)
    same = owner_col == owner_row
    rank_row = jnp.sum(jnp.where(same & (at0 < at1), 1.0, 0.0), axis=0, keepdims=True)
    rank_col = jnp.sum(jnp.where(same & (at1 < at0), 1.0, 0.0), axis=1, keepdims=True)
    target_row = jnp.where(slot_row >= 0.0, owner_row * CAP + rank_row, -1.0)
    target_col = jnp.where(slot_col >= 0.0, owner_col * CAP + rank_col, -1.0)
    hit = iota((NS * CAP, POS), 0).astype(F32) == target_row
    pick = jnp.where(hit, 1.0, 0.0).astype(BF)
    loads[0].wait()
    for p in range(NP):
        rs[p] = mm(pick, llm_ref[:, PW * p : PW * p + PW], 1, 0).astype(BF).reshape(NS, CAP, PW)
    lane = iota((1, 128), 1)
    lane_slot = (lane % CAP).astype(F32)
    mine = lane // CAP == s % 4
    landing = slot_col - owner_col * TOK + 1.0
    for o in range(NS):
        found = jnp.where((target_col == lane_slot + float(o * CAP)) & mine, landing, 0.0)
        ids[o] = jnp.sum(found, axis=0, keepdims=True) - 1.0
    ngain_col = to_column(ngain_ref[...].astype(F32))
    place_gain = iota((ROWS_DP, D), 1) == iota((ROWS_DP, D), 0) + d * ROWS_DP
    gsh[...] = jnp.sum(jnp.where(place_gain, ngain_col, 0.0), axis=0, keepdims=True)

    pl.semaphore_wait(barrier, NS + ND - 2 + 2 * c - jnp.where(own_final, 1, 0))

    def gain_copy(k):
        return remote(gsh, gr.at[d], "gr", k, s, (d + k) % ND)

    def row_copy(p, k):
        to = (s + k) % NS
        return remote(rs.at[p, to], rr.at[p, s], "rr", p * NS + k, to, d)

    def id_copy(k):
        to = (s + k) % NS
        return remote(ids.at[to], ri.at[s], "ri", k, to, d)

    far_first = (8, 7, 9, 6, 10, 5, 11, 4, 12, 3, 13, 2, 14, 1, 15)
    for k in far_first:
        id_copy(k).start()
    for k in far_first:
        row_copy(0, k).start()
    for k in range(1, ND):
        gain_copy(k).start()

    def quarter(q):
        return wup_ref.at[:, pl.ds(pl.multiple_of(q * FQ, 128), FQ)]

    def wy_copy(k):
        return remote(quarter((y + k) % NY), wu.at[y, x], "wy", k, s, y_peer(k))

    def ux_copy(k):
        return remote(wu.at[:, x], wu.at[:, x], "wx", k, s, x_peer(k))

    def dx_copy(k):
        return remote(wd.at[x], wd.at[x], "wx", k, s, x_peer(k))

    def ul_copy(k):
        at = (x + NX - k) % NX
        return remote(wu.at[:, at], wu.at[:, at], "rl", k, s + 1, d)

    def dl_copy(k):
        at = (x + NX - k) % NX
        return remote(wd.at[at], wd.at[at], "rl", k, s - 1, d)

    own_up = pltpu.make_async_copy(quarter(y), wu.at[y, x], s_loc.at[0])
    own_down = pltpu.make_async_copy(wdown_ref, wd.at[x], s_loc.at[1])

    @pl.when(c == 0)
    def _():
        for k in (2, 1, 3):
            wy_copy(k).start()
        own_up.start()
        own_up.wait()

    @pl.when(c == 1)
    def _():
        own_down.start()
        own_down.wait()
        for k in (2, 1, 3):
            dx_copy(k).start()
        dl_copy(0).start()

    for p in range(1, NP):
        for k in far_first:
            row_copy(p, k).start()
    for p in range(NP):
        rr[p, s] = rs[p, s]
    ri[s] = ids[s]

    row_late = iota((TOK, TOK), 0) >= BLK
    col_late = iota((TOK, TOK), 1) >= BLK
    flags = [[mask_ref[0, i : i + 1, j : j + 1] for j in range(2)] for i in range(2)]
    allowed = (
        jnp.where(
            row_late,
            jnp.where(col_late, flags[1][1], flags[1][0]),
            jnp.where(col_late, flags[0][1], flags[0][0]),
        )
        > 0
    )

    def window(h):
        first, last = HDIM * h // 128, (HDIM * h + HDIM - 1) // 128
        lanes = slice(128 * first, 128 * last + 128)
        feature = iota((1, lanes.stop - lanes.start), 1) + lanes.start
        inside = (feature >= HDIM * h) & (feature < HDIM * h + HDIM)
        return lanes, jnp.where(inside, 1.0, 0.0).astype(BF)

    class Tiles:
        def __init__(self, out):
            self.out, self.open = out, {}

        def add(self, h, value):
            first = HDIM * h // 128
            for i in range(value.shape[1] // 128):
                part = value[:, 128 * i : 128 * i + 128]
                held = self.open.get(first + i)
                self.open[first + i] = part if held is None else held + part
            upto = HDIM * (h + 1) // 128 if h + 1 < HEADS else D // 128
            for t in [t for t in self.open if t < upto]:
                self.out[:, 128 * t : 128 * t + 128] = self.open.pop(t).astype(BF)

    att_tiles = Tiles(att)

    def attend(h):
        lanes, inside = window(h)
        scores = mm(q_ref[:, lanes], k_ref[:, lanes] * inside, 1, 1) * scale
        masked = jnp.where(allowed, scores, -jnp.inf)
        highest = jnp.max(masked, axis=1, keepdims=True)
        terms = jnp.where(allowed, jnp.exp(masked - highest), 0.0)
        prob = terms * (1.0 / jnp.sum(terms, axis=1, keepdims=True))
        probs[h] = prob
        att_tiles.add(h, mm(prob.astype(BF), v_ref[:, lanes] * inside, 1, 0))

    for copy in loads[1:]:
        copy.wait()
    for h in range(HEADS // 2):
        attend(h)

    @pl.when(c == 0)
    def _():
        for k in range(1, NY):
            wy_copy(k).wait_recv()
        for k in (2, 1, 3):
            ux_copy(k).start()
        ul_copy(0).start()

    for h in range(HEADS // 2, HEADS):
        attend(h)

    gr[d] = gsh[...]
    for k in range(1, ND):
        gain_copy(k).wait_recv()
    gain_full = jnp.sum(gr[...], axis=0)

    def unit_step(i, carry):
        rows = pl.ds(pl.multiple_of(i * 32, 32), 32)
        hidden = resid_ref[rows, :].astype(F32) + att[rows, :].astype(F32)
        center = jnp.mean(hidden, axis=1, keepdims=True)
        away = hidden - center
        inverse = lax.rsqrt(jnp.mean(away * away, axis=1, keepdims=True) + 1e-06)
        inv[rows, :] = inverse
        out = away * inverse
        unit[rows, :] = out
        ra[0, y, rows, :] = (out * gain_full).astype(BF)
        return carry

    lax.fori_loop(0, TOK // 32, unit_step, 0)

    def na_copy(k):
        return remote(ra.at[0, y], ra.at[0, y], "na", k, s, y_peer(k))

    for k in (1, 3):
        na_copy(k).start()

    def nf_copy(way):
        at = (y + NY - 1) % NY if way == 0 else (y + 1) % NY
        view = ra.at[0, at, pl.ds(way * BLK, BLK)]
        return remote(view, view, "nf", way, s, y_peer(1 if way == 0 else 3))

    def n_forward():
        for way, k in ((0, 1), (1, 3)):
            na_copy(k).wait_recv()
            nf_copy(way).start()

    @pl.when(c == 1)
    def _():
        for k in (1, 3, 2):
            dx_copy(k).wait_recv()
            dl_copy(k).start()

    for k in range(1, NS):
        id_copy(k).wait_recv()
    token = iota((TOK, 128), 0).astype(F32)
    place = jnp.concatenate(
        [
            jnp.where(token == jnp.max(ri[4 * j : 4 * j + 4], axis=0), 1.0, 0.0).astype(BF)
            for j in range(4)
        ],
        axis=1,
    )

    def piece(p):
        return slice(PW * p, PW * p + PW)

    def ga_copy(p, k):
        view = ra.at[1, y, :, piece(p)]
        return remote(view, view, "ga", p * NY + k, s, y_peer(k))

    def gf_copy(p, way):
        at = (y + NY - 1) % NY if way == 0 else (y + 1) % NY
        view = ra.at[1, at, pl.ds(way * BLK, BLK), piece(p)]
        return remote(view, view, "gf", p * 2 + way, s, y_peer(1 if way == 0 else 3))

    def rows_in(p):
        for k in range(1, NS):
            row_copy(p, k).wait_recv()
        ra[1, y, :, piece(p)] = mm(place, rr[p].reshape(NS * CAP, PW), 1, 0).astype(BF)
        for k in (1, 3) if p < NP - 1 else (2, 1, 3):
            ga_copy(p, k).start()
        if p > 0:
            for way, k in ((0, 1), (1, 3)):
                ga_copy(p - 1, k).wait_recv()
                gf_copy(p - 1, way).start()

    rows_in(0)
    rows_in(1)
    n_forward()
    rows_in(2)

    @pl.when(c == 0)
    def _():
        for k in (1, 3, 2):
            ux_copy(k).wait_recv()
            ul_copy(k).start()

    @pl.when(c == 1)
    def _():
        for k in range(NX):
            ul_copy(k).wait_recv()

    for way in range(2):
        nf_copy(way).wait_recv()
    half = 2 * TOK

    def up_step(i, carry):
        rows = pl.ds(pl.multiple_of(i * half, half), half)
        pre = mm(ra[0, pl.ds(2 * i, 2)].reshape(half, D), wu[...].reshape(D, FQ), 1, 0)
        sig = jax.nn.sigmoid(1.702 * pre)
        la[1, rows, :] = (pre * sig).astype(BF)
        gate[rows, :] = sig + 1.702 * pre * sig * (1.0 - sig)
        return carry

    lax.fori_loop(0, 2, up_step, 0)

    rows_in(3)
    rows_in(4)

    @pl.when(c == 0)
    def _():
        for k in range(NX):
            dl_copy(k).wait_recv()

    def cd_copy(p):
        return remote(gt.at[1, :, piece(p)], cr.at[:, piece(p)], "c", p, s + 1, d)

    def cu_copy(i):
        rows = slice(128 * i, 128 * i + 128)
        return remote(gt.at[0, rows], cr.at[rows], "c", i, s - 1, d)

    def down_in(p):
        cd_copy(p).wait_recv()
        xs[:, piece(p)] = (
            gt[1, :, piece(p)].astype(F32) + cr[:, piece(p)].astype(F32)
        ).astype(BF)

    for k in range(1, NS):
        for p in range(NP):
            row_copy(p, k).wait_send()
        id_copy(k).wait_send()
    for k in range(1, ND):
        gain_copy(k).wait_send()

    for p in range(NP):
        if p < NP - 1:
            for way in range(2):
                gf_copy(p, way).wait_recv()
        else:
            for k in range(1, NY):
                ga_copy(p, k).wait_recv()
        grads = ra[1, :, :, piece(p)].reshape(NY * TOK, PW)
        part = mm(grads, wd[:, :, piece(p)].reshape(FQ, PW), 1, 1)
        dact[...] = part if p == 0 else dact[...] + part
        gt[1, :, piece(p)] = mm(la[1], grads, 0, 0).astype(BF)

        @pl.when(c == 0)
        def _(p=p):
            cd_copy(p).start()

        if p > 0:

            @pl.when(c == 1)
            def _(p=p):
                down_in(p - 1)

    la[0] = (dact[...] * gate[...]).astype(BF)

    def x_copy(r, k):
        to = (x + k) % NX
        rows = pl.ds(pl.multiple_of(to * FF_DP + r * RW, RW), RW)
        return remote(
            xs.at[rows], xr.at[x, pl.ds(r * RW, RW)], "x", r * NX + k, s, y * NX + to
        )

    @pl.when(c == 1)
    def _():
        down_in(NP - 1)
        for r in range(NR):
            for k in (2, 1, 3):
                x_copy(r, k).start()

    def norm_step(i, acc):
        rows = pl.ds(pl.multiple_of(i * half, half), half)
        part = mm(la[0, rows, :], wu[...].reshape(D, FQ), 1, 1)
        dns[pl.ds(2 * i, 2)] = part.astype(BF).reshape(2, TOK, D)
        normed = ra[0, pl.ds(2 * i, 2)].reshape(half, D).astype(F32)
        return acc + jnp.sum(part * normed, axis=0, keepdims=True)

    gp[...] = lax.fori_loop(0, 2, norm_step, jnp.zeros((1, D), F32))

    def dn_copy(k):
        to = (y + k) % NY
        return remote(dns.at[to], dnr.at[y], "dn", k, s, to * NX + x)

    for k in (2, 1, 3):
        dn_copy(k).start()

    def g1_copy(k):
        return remote(gp, gs1.at[s], "g1", k, (s + k) % NS, d)

    for k in range(1, NS):
        g1_copy(k).start()

    for i in range(FQ // 128):
        rows = slice(128 * i, 128 * i + 128)
        gt[0, rows, :] = mm(la[0, :, rows], ra[0].reshape(NY * TOK, D), 0, 0).astype(BF)

        @pl.when(c == 1)
        def _(i=i):
            cu_copy(i).start()

    @pl.when(c == 0)
    def _():
        for i in range(FQ // 128):
            cu_copy(i).wait_recv()
        for r in range(NR):
            for b in range(NX):
                rows = pl.ds(b * FF_DP + r * RW, RW)
                xs[rows, :] = (gt[0, rows, :].astype(F32) + cr[rows, :].astype(F32)).astype(BF)
            for k in (2, 1, 3):
                x_copy(r, k).start()

    def z_copy(r, k):
        to = (z + k) % NZ
        rows = pl.ds(r * RW, RW)
        return remote(
            zs.at[rows, pl.ds(window_start(to), WIN)],
            zr.at[z, rows],
            "z",
            r * NZ + k,
            2 * to + c,
            d,
        )

    for r in range(NR):
        rows = pl.ds(r * RW, RW)
        own = pl.ds(pl.multiple_of(x * FF_DP + r * RW, RW), RW)
        for k in range(1, NX):
            x_copy(r, k).wait_recv()
        xr[x, rows] = xs[own, :]
        zs[rows, :] = jnp.sum(xr[:, rows, :].astype(F32), axis=0).astype(BF)
        for k in (4, 3, 5, 2, 6, 1, 7):
            z_copy(r, k).start()
        zr[z, rows] = zs[rows, pl.ds(window_start(z), WIN)]

    gs1[s] = gp[...]
    for k in range(1, NS):
        g1_copy(k).wait_recv()
    gp2[...] = jnp.sum(gs1[...], axis=0)

    def g2_copy(k):
        return remote(gp2, gs2.at[d], "g2", k, s, (d + k) % ND)

    for k in range(1, ND):
        g2_copy(k).start()

    dnr[y] = dns[y]
    for k in range(1, NY):
        dn_copy(k).wait_recv()
    gain_again = jnp.sum(gr[...], axis=0)

    def resid_step(i, carry):
        rows = pl.ds(pl.multiple_of(i * 32, 32), 32)
        d_unit = jnp.sum(dnr[:, rows, :].astype(F32), axis=0) * gain_again
        normal = unit[rows, :]
        first = jnp.mean(d_unit, axis=1, keepdims=True)
        second = jnp.mean(d_unit * normal, axis=1, keepdims=True)
        d_hidden = inv[rows, :] * (d_unit - first - normal * second)
        gresid_ref[rows, :] = (ra[1, y, rows, :].astype(F32) + d_hidden).astype(BF)
        return carry

    lax.fori_loop(0, TOK // 32, resid_step, 0)

    stores[0].start()
    gq_tiles, gk_tiles, gv_tiles = Tiles(gq_ref), Tiles(gk_ref), Tiles(gv_ref)
    for h in range(HEADS):
        lanes, inside = window(h)
        grad = gresid_ref[:, lanes] * inside
        prob = probs[h]
        gv_tiles.add(h, mm(prob.astype(BF), grad, 0, 0))
        d_probs = mm(grad, v_ref[:, lanes], 1, 1)
        delta = jnp.sum(
            grad.astype(F32) * att[:, lanes].astype(F32), axis=1, keepdims=True
        )
        d_scores = (prob * (d_probs - delta) * scale).astype(BF)
        gq_tiles.add(h, mm(d_scores, k_ref[:, lanes] * inside, 1, 0))
        gk_tiles.add(h, mm(d_scores, q_ref[:, lanes] * inside, 0, 0))
    for copy in stores[1:]:
        copy.start()

    factor = 1.0 / math.sqrt(NS * ND * TOK)
    gs2[d] = gp2[...]
    for k in range(1, ND):
        g2_copy(k).wait_recv()
    ggain_ref[...] = jnp.sum(gs2[...], axis=0) * factor / gain_again

    for r in range(NR):
        for k in range(1, NZ):
            z_copy(r, k).wait_recv()
    fs[...] = (jnp.sum(zr[...].astype(F32), axis=0) * factor).astype(BF)

    u_copy = remote(fs, fu, "f", 0, s + 1, d)
    d0_copy = remote(fs, fd, "f", 1, d, 2 * z)
    d1_copy = remote(fs, fd, "f", 2, d, 2 * z + 1, 1)
    own_down_out = pltpu.make_async_copy(fs, fd, s_loc.at[2])

    def chosen(first):
        return jnp.where(
            iota((ROWS_DP, WIN), 1) == iota((ROWS_DP, WIN), 0) + first, 1.0, 0.0
        ).astype(BF)

    own_lanes = chosen(32 * (z % 4) + ROWS_DP * c)

    @pl.when(c == 0)
    def _():
        u_copy.start()
        up_ref[...] = mm(own_lanes, fs[...], 1, 1).astype(BF)

    @pl.when(c == 1)
    def _():
        d0_copy.start()

        @pl.when(s == d)
        def _():
            own_down_out.start()
            own_down_out.wait()

        @pl.when(s != d)
        def _():
            d1_copy.start()

        u_copy.wait_recv()
        up_ref[...] = mm(own_lanes, fu[...], 1, 1).astype(BF)

    @pl.when(jnp.logical_not(own_final))
    def _():
        d0_copy.wait_recv()

    down_ref[...] = mm(
        fd[...], chosen(32 * ((d // 2) % 4) + ROWS_DP * (d % 2)), 1, 1
    ).astype(BF)

    @pl.when(c == 0)
    def _():
        u_copy.wait_send()
        for k in range(1, NY):
            wy_copy(k).wait_send()
        for k in range(1, NX):
            ux_copy(k).wait_send()
        for k in range(NX):
            ul_copy(k).wait_send()
        for p in range(NP):
            cd_copy(p).wait_send()

    @pl.when(c == 1)
    def _():
        d0_copy.wait_send()

        @pl.when(s != d)
        def _():
            d1_copy.wait_send()

        for k in range(1, NX):
            dx_copy(k).wait_send()
        for k in range(NX):
            dl_copy(k).wait_send()
        for i in range(FQ // 128):
            cu_copy(i).wait_send()

    for k in range(1, NS):
        g1_copy(k).wait_send()
    for k in range(1, ND):
        g2_copy(k).wait_send()
    for k in range(1, NY):
        if k != 2:
            na_copy(k).wait_send()
        for p in range(NP):
            if k != 2 or p == NP - 1:
                ga_copy(p, k).wait_send()
        dn_copy(k).wait_send()
    for way in range(2):
        nf_copy(way).wait_send()
        for p in range(NP - 1):
            gf_copy(p, way).wait_send()
    for copy in stores:
        copy.wait()
    for r in range(NR):
        for k in range(1, NX):
            x_copy(r, k).wait_send()
        for k in range(1, NZ):
            z_copy(r, k).wait_send()


def layer(*args):
    vm = pl.BlockSpec(memory_space=pltpu.VMEM)
    hbm = pl.BlockSpec(memory_space=pl.ANY)
    sem = pltpu.SemaphoreType.DMA
    sems = [sem((12,))]
    for n in SEMS.values():
        sems += [sem((n,)), sem((n,))]
    out = jax.ShapeDtypeStruct
    return pl.pallas_call(
        kernel,
        out_shape=(
            out((TOK, D), BF),
            out((TOK, D), BF),
            out((TOK, D), BF),
            out((TOK, D), BF),
            out((ROWS_DP, FF_DP), BF),
            out((FF_DP, ROWS_DP), BF),
            out((1, D), F32),
        ),
        in_specs=[hbm] * 5 + [vm, vm, hbm, hbm, vm],
        out_specs=(hbm,) * 4 + (vm,) * 3,
        scratch_shapes=[
            *[pltpu.VMEM((TOK, D), BF)] * 4,
            pltpu.VMEM((POS, D), BF),
            *[pltpu.VMEM((TOK, D), BF)] * 4,
            pltpu.VMEM((NP, NS, CAP, PW), BF),
            pltpu.VMEM((NP, NS, CAP, PW), BF),
            pltpu.VMEM((NS, 1, 128), F32),
            pltpu.VMEM((NS, 1, 128), F32),
            pltpu.VMEM((1, D), F32),
            pltpu.VMEM((ND, 1, D), F32),
            pltpu.VMEM((NY, NX, ROWS_DP, FQ), BF),
            pltpu.VMEM((NX, FF_DP, D), BF),
            pltpu.VMEM((2, NY, TOK, D), BF),
            pltpu.VMEM((2, NY * TOK, FQ), BF),
            pltpu.VMEM((NY * TOK, FQ), F32),
            pltpu.VMEM((NY * TOK, FQ), F32),
            pltpu.VMEM((NY, TOK, D), BF),
            pltpu.VMEM((NY, TOK, D), BF),
            pltpu.VMEM((2, FQ, D), BF),
            pltpu.VMEM((FQ, D), BF),
            pltpu.VMEM((FQ, D), BF),
            pltpu.VMEM((NX, FF_DP, D), BF),
            pltpu.VMEM((FF_DP, D), BF),
            pltpu.VMEM((NZ, FF_DP, WIN), BF),
            pltpu.VMEM((FF_DP, WIN), BF),
            pltpu.VMEM((FF_DP, WIN), BF),
            pltpu.VMEM((FF_DP, WIN), BF),
            pltpu.VMEM((1, D), F32),
            pltpu.VMEM((NS, 1, D), F32),
            pltpu.VMEM((1, D), F32),
            pltpu.VMEM((ND, 1, D), F32),
            pltpu.VMEM((HEADS, TOK, TOK), F32),
            pltpu.VMEM((TOK, D), BF),
            pltpu.VMEM((TOK, D), F32),
            pltpu.VMEM((TOK, 1), F32),
            *sems,
        ],
        compiler_params=pltpu.CompilerParams(
            collective_id=0, has_side_effects=True, vmem_limit_bytes=56 * 2**20
        ),
    )(*args)


def hand_out_kernel(*refs):
    n = 7
    ins, outs, held, taken, done = refs[:n], refs[n : 2 * n], refs[2 * n : -2], refs[-2], refs[-1]
    into = [pltpu.make_async_copy(ins[i], held[i], taken.at[i]) for i in range(4)]
    out = [
        pltpu.make_async_copy(held[i] if i < 4 else ins[i], outs[i], done.at[i])
        for i in range(n - 1)
    ]
    for copy in into:
        copy.start()
    for copy in out[4:]:
        copy.start()
    outs[n - 1][...] = ins[n - 1][0, :]
    for i in range(4):
        into[i].wait()
        out[i].start()
    for copy in out:
        copy.wait()


def hand_out(arrays):
    vm = pl.BlockSpec(memory_space=pltpu.VMEM)
    hbm = pl.BlockSpec(memory_space=pl.ANY)
    return pl.pallas_call(
        hand_out_kernel,
        out_shape=tuple(jax.ShapeDtypeStruct(a.shape, a.dtype) for a in arrays[:-1])
        + (jax.ShapeDtypeStruct((D,), F32),),
        in_specs=[hbm] * 4 + [vm] * 3,
        out_specs=(hbm,) * 6 + (vm,),
        scratch_shapes=[
            *[pltpu.VMEM((TOK, D), BF)] * 4,
            pltpu.SemaphoreType.DMA((4,)),
            pltpu.SemaphoreType.DMA((6,)),
        ],
    )(*arrays)


def per_device(
    queries, key_rows, value_rows, resid_in, llm_grad, vision_slot, window_mask, w_up, w_down,
    norm_gain,
):
    results = layer(
        queries[0],
        key_rows[0],
        value_rows[0],
        resid_in[0],
        llm_grad[0],
        vision_slot,
        window_mask,
        w_up,
        w_down,
        norm_gain.reshape(1, ROWS_DP),
    )
    grad_query, grad_key, grad_value, grad_resid, grad_up, grad_down, grad_gain = hand_out(results)
    return (
        grad_query[None],
        grad_key[None],
        grad_value[None],
        grad_resid[None],
        grad_up,
        grad_down,
        grad_gain,
    )


def solution(mesh):
    row3 = P("dp", "seq", None)
    in_specs = (
        row3,
        row3,
        row3,
        row3,
        row3,
        P("dp", "seq"),
        row3,
        P("dp", None),
        P("dp", None),
        P("dp"),
    )
    out_specs = (row3, row3, row3, row3, P("seq", "dp"), P("seq", "dp"), P())
    return jax.shard_map(
        per_device, mesh=mesh, in_specs=in_specs, out_specs=out_specs, check_vma=False
    )
```

```python
import math

import jax
import jax.numpy as jnp
from jax import lax
from jax.experimental import pallas as pl
from jax.experimental.pallas import tpu as pltpu
from jax.sharding import PartitionSpec as P

HEADS = 16
HDIM = 80
BLK = 64
D = 1280
FF = 2560
TOK = 128
POS = 192
NS = 16
ND = 16
CAP = 32
NY, NX, NZ = 4, 4, 8
FQ = FF // NY
ROWS_DP = D // ND
FF_DP = FF // ND
WIN = 256
NP = 5
PW = D // NP
NRELAY = 3
NR = 5
RW = FF_DP // NR
WHOLE = ((0,), (1, 2), (3,), (4, 5), (6, 7))
MESH = pl.DeviceIdType.MESH
BF = jnp.bfloat16
F32 = jnp.float32


def mm(left, right, left_dim, right_dim):
    return lax.dot_general(
        left, right, (((left_dim,), (right_dim,)), ((), ())), preferred_element_type=F32
    )


def iota(shape, dim):
    return lax.broadcasted_iota(jnp.int32, shape, dim)


def to_column(row):
    n = row.shape[1]
    same = iota((n, n), 0) == iota((n, n), 1)
    return jnp.sum(jnp.where(same, row, 0.0), axis=1, keepdims=True)


def window_start(z):
    return pl.multiple_of(128 * ((5 * z) // 4), 128)


SEMS = {
    "gr": ND, "rr": NP * NS, "ri": NS, "wy": NY, "wx": NX, "rl": NX, "na": NY, "nf": 2, "ga": NP * NY, "gf": NP * 2,
    "dn": NY, "c": 5, "x": NR * NX, "z": NR * NZ, "f": 3, "g1": NS, "g2": ND,
}


def kernel(
    q_hbm, k_hbm, v_hbm, resid_hbm, llm_hbm, slot_ref, mask_ref, wup_ref, wdown_ref, ngain_ref,
    gq_hbm, gk_hbm, gv_hbm, gresid_hbm, up_ref, down_ref, ggain_ref,
    q_ref, k_ref, v_ref, resid_ref, llm_ref, gq_ref, gk_ref, gv_ref, gresid_ref,
    rs, rr, ids, ri, gsh, gr, wu, wd, ra, la, gate, dact, dns, dnr, gt, cr, xs, xr, zs, zr,
    fs, fu, fd, gp, gs1, gp2, gs2, probs, att, unit, inv, s_loc, *sems,
):
    names = list(SEMS)
    send = {n: sems[2 * i] for i, n in enumerate(names)}
    recv = {n: sems[2 * i + 1] for i, n in enumerate(names)}
    s = lax.axis_index("seq")
    d = lax.axis_index("dp")
    z, c = s // 2, s % 2
    y, x = d // NX, d % NX
    scale = 1.0 / math.sqrt(HDIM)

    def remote(src, dst, name, at, to_s, to_d, at_recv=None):
        return pltpu.make_async_remote_copy(
            src_ref=src,
            dst_ref=dst,
            send_sem=send[name].at[at],
            recv_sem=recv[name].at[at if at_recv is None else at_recv],
            device_id=(to_s, to_d),
            device_id_type=MESH,
        )

    def y_peer(k):
        return ((y + k) % NY) * NX + x

    def x_peer(k):
        return y * NX + (x + k) % NX

    def local(src, dst, at):
        return pltpu.make_async_copy(src, dst, s_loc.at[at])

    loads = [
        local(llm_hbm, llm_ref, 3),
        local(q_hbm, q_ref, 4),
        local(k_hbm, k_ref, 5),
        local(v_hbm, v_ref, 6),
        local(resid_hbm, resid_ref, 7),
    ]
    stores = [
        local(gresid_ref, gresid_hbm, 8),
        local(gq_ref, gq_hbm, 9),
        local(gk_ref, gk_hbm, 10),
        local(gv_ref, gv_hbm, 11),
    ]
    for copy in loads:
        copy.start()

    barrier = pltpu.get_barrier_semaphore()
    for k in range(1, NS):
        pl.semaphore_signal(barrier, inc=1, device_id=((s + k) % NS, d), device_id_type=MESH)
    for k in range(1, ND):
        pl.semaphore_signal(barrier, inc=1, device_id=(s, (d + k) % ND), device_id_type=MESH)
    from_s = 2 * (d // 2) + 1
    own_final = jnp.logical_and(from_s == s, s == d)

    @pl.when(jnp.logical_not(own_final))
    def _():
        pl.semaphore_signal(barrier, inc=1, device_id=(from_s, s), device_id_type=MESH)

    slot_row = slot_ref[...].astype(F32)
    slot_col = to_column(slot_row)
    owner_row = jnp.floor(slot_row * (1.0 / TOK))
    owner_col = jnp.floor(slot_col * (1.0 / TOK))
    at0, at1 = iota((POS, POS), 0), iota((POS, POS), 1)
    same = owner_col == owner_row
    rank_row = jnp.sum(jnp.where(same & (at0 < at1), 1.0, 0.0), axis=0, keepdims=True)
    rank_col = jnp.sum(jnp.where(same & (at1 < at0), 1.0, 0.0), axis=1, keepdims=True)
    target_row = jnp.where(slot_row >= 0.0, owner_row * CAP + rank_row, -1.0)
    target_col = jnp.where(slot_col >= 0.0, owner_col * CAP + rank_col, -1.0)
    hit = iota((NS * CAP, POS), 0).astype(F32) == target_row
    pick = jnp.where(hit, 1.0, 0.0).astype(BF)
    loads[0].wait()
    for p in range(NP):
        rs[p] = mm(pick, llm_ref[:, PW * p : PW * p + PW], 1, 0).astype(BF).reshape(NS, CAP, PW)
    lane = iota((1, 128), 1)
    lane_slot = (lane % CAP).astype(F32)
    mine = lane // CAP == s % 4
    landing = slot_col - owner_col * TOK + 1.0
    for o in range(NS):
        found = jnp.where((target_col == lane_slot + float(o * CAP)) & mine, landing, 0.0)
        ids[o] = jnp.sum(found, axis=0, keepdims=True) - 1.0
    ngain_col = to_column(ngain_ref[...].astype(F32))
    place_gain = iota((ROWS_DP, D), 1) == iota((ROWS_DP, D), 0) + d * ROWS_DP
    gsh[...] = jnp.sum(jnp.where(place_gain, ngain_col, 0.0), axis=0, keepdims=True)

    pl.semaphore_wait(barrier, NS + ND - 2 + 2 * c - jnp.where(own_final, 1, 0))

    def gain_copy(k):
        return remote(gsh, gr.at[d], "gr", k, s, (d + k) % ND)

    def row_copy(p, k):
        to = (s + k) % NS
        return remote(rs.at[p, to], rr.at[p, s], "rr", p * NS + k, to, d)

    def id_copy(k):
        to = (s + k) % NS
        return remote(ids.at[to], ri.at[s], "ri", k, to, d)

    far_first = (8, 7, 9, 6, 10, 5, 11, 4, 12, 3, 13, 2, 14, 1, 15)
    for k in far_first:
        id_copy(k).start()
    for k in far_first:
        row_copy(0, k).start()
    for k in range(1, ND):
        gain_copy(k).start()

    def quarter(q):
        return wup_ref.at[:, pl.ds(pl.multiple_of(q * FQ, 128), FQ)]

    def wy_copy(k):
        return remote(quarter((y + k) % NY), wu.at[y, x], "wy", k, s, y_peer(k))

    def ux_copy(k):
        return remote(wu.at[:, x], wu.at[:, x], "wx", k, s, x_peer(k))

    def dx_copy(k):
        return remote(wd.at[x], wd.at[x], "wx", k, s, x_peer(k))

    def ul_copy(k):
        at = (x + NX - k) % NX
        return remote(wu.at[:, at], wu.at[:, at], "rl", k, s + 1, d)

    def dl_copy(k):
        at = (x + NX - k) % NX
        return remote(wd.at[at], wd.at[at], "rl", k, s - 1, d)

    own_up = pltpu.make_async_copy(quarter(y), wu.at[y, x], s_loc.at[0])
    own_down = pltpu.make_async_copy(wdown_ref, wd.at[x], s_loc.at[1])

    @pl.when(c == 0)
    def _():
        for k in (2, 1, 3):
            wy_copy(k).start()
        own_up.start()
        own_up.wait()

    @pl.when(c == 1)
    def _():
        own_down.start()
        own_down.wait()
        for k in (2, 1, 3):
            dx_copy(k).start()
        dl_copy(0).start()

    for p in range(1, NP):
        for k in far_first:
            row_copy(p, k).start()
    for p in range(NP):
        rr[p, s] = rs[p, s]
    ri[s] = ids[s]

    row_late = iota((TOK, TOK), 0) >= BLK
    col_late = iota((TOK, TOK), 1) >= BLK
    flags = [[mask_ref[0, i : i + 1, j : j + 1] for j in range(2)] for i in range(2)]
    allowed = (
        jnp.where(
            row_late,
            jnp.where(col_late, flags[1][1], flags[1][0]),
            jnp.where(col_late, flags[0][1], flags[0][0]),
        )
        > 0
    )

    def window(h):
        first, last = HDIM * h // 128, (HDIM * h + HDIM - 1) // 128
        lanes = slice(128 * first, 128 * last + 128)
        feature = iota((1, lanes.stop - lanes.start), 1) + lanes.start
        inside = (feature >= HDIM * h) & (feature < HDIM * h + HDIM)
        return lanes, jnp.where(inside, 1.0, 0.0).astype(BF)

    class Tiles:
        def __init__(self, out):
            self.out, self.open = out, {}

        def add(self, h, value):
            first = HDIM * h // 128
            for i in range(value.shape[1] // 128):
                part = value[:, 128 * i : 128 * i + 128]
                held = self.open.get(first + i)
                self.open[first + i] = part if held is None else held + part
            upto = HDIM * (h + 1) // 128 if h + 1 < HEADS else D // 128
            for t in [t for t in self.open if t < upto]:
                self.out[:, 128 * t : 128 * t + 128] = self.open.pop(t).astype(BF)

    att_tiles = Tiles(att)

    def attend(h):
        lanes, inside = window(h)
        scores = mm(q_ref[:, lanes], k_ref[:, lanes] * inside, 1, 1) * scale
        masked = jnp.where(allowed, scores, -jnp.inf)
        highest = jnp.max(masked, axis=1, keepdims=True)
        terms = jnp.where(allowed, jnp.exp(masked - highest), 0.0)
        prob = terms * (1.0 / jnp.sum(terms, axis=1, keepdims=True))
        probs[h] = prob
        att_tiles.add(h, mm(prob.astype(BF), v_ref[:, lanes] * inside, 1, 0))

    for copy in loads[1:]:
        copy.wait()
    for h in range(HEADS // 2):
        attend(h)

    @pl.when(c == 0)
    def _():
        for k in range(1, NY):
            wy_copy(k).wait_recv()
        for k in (2, 1, 3):
            ux_copy(k).start()
        ul_copy(0).start()

    for h in range(HEADS // 2, HEADS):
        attend(h)

    gr[d] = gsh[...]
    for k in range(1, ND):
        gain_copy(k).wait_recv()
    gain_full = jnp.sum(gr[...], axis=0)

    def unit_step(i, carry):
        rows = pl.ds(pl.multiple_of(i * 32, 32), 32)
        hidden = resid_ref[rows, :].astype(F32) + att[rows, :].astype(F32)
        center = jnp.mean(hidden, axis=1, keepdims=True)
        away = hidden - center
        inverse = lax.rsqrt(jnp.mean(away * away, axis=1, keepdims=True) + 1e-06)
        inv[rows, :] = inverse
        out = away * inverse
        unit[rows, :] = out
        ra[0, y, rows, :] = (out * gain_full).astype(BF)
        return carry

    lax.fori_loop(0, TOK // 32, unit_step, 0)

    def na_copy(k):
        return remote(ra.at[0, y], ra.at[0, y], "na", k, s, y_peer(k))

    for k in (1, 3):
        na_copy(k).start()

    def nf_copy(way):
        at = (y + NY - 1) % NY if way == 0 else (y + 1) % NY
        view = ra.at[0, at, pl.ds(way * BLK, BLK)]
        return remote(view, view, "nf", way, s, y_peer(1 if way == 0 else 3))

    def n_forward():
        for way, k in ((0, 1), (1, 3)):
            na_copy(k).wait_recv()
            nf_copy(way).start()

    @pl.when(c == 1)
    def _():
        for k in (1, 3, 2):
            dx_copy(k).wait_recv()
            dl_copy(k).start()

    for k in range(1, NS):
        id_copy(k).wait_recv()
    token = iota((TOK, 128), 0).astype(F32)
    place = jnp.concatenate(
        [
            jnp.where(token == jnp.max(ri[4 * j : 4 * j + 4], axis=0), 1.0, 0.0).astype(BF)
            for j in range(4)
        ],
        axis=1,
    )

    def piece(p):
        return slice(PW * p, PW * p + PW)

    def ga_copy(p, k):
        view = ra.at[1, y, :, piece(p)]
        return remote(view, view, "ga", p * NY + k, s, y_peer(k))

    def gf_copy(p, way):
        at = (y + NY - 1) % NY if way == 0 else (y + 1) % NY
        view = ra.at[1, at, pl.ds(way * BLK, BLK), piece(p)]
        return remote(view, view, "gf", p * 2 + way, s, y_peer(1 if way == 0 else 3))

    def rows_in(p):
        for k in range(1, NS):
            row_copy(p, k).wait_recv()
        ra[1, y, :, piece(p)] = mm(place, rr[p].reshape(NS * CAP, PW), 1, 0).astype(BF)
        for k in (1, 3) if p < NRELAY else (2, 1, 3):
            ga_copy(p, k).start()
        if 0 < p <= NRELAY:
            for way, k in ((0, 1), (1, 3)):
                ga_copy(p - 1, k).wait_recv()
                gf_copy(p - 1, way).start()

    rows_in(0)
    rows_in(1)
    n_forward()
    rows_in(2)

    @pl.when(c == 0)
    def _():
        for k in (1, 3, 2):
            ux_copy(k).wait_recv()
            ul_copy(k).start()

    @pl.when(c == 1)
    def _():
        for k in range(NX):
            ul_copy(k).wait_recv()

    for way in range(2):
        nf_copy(way).wait_recv()
    half = 2 * TOK

    def up_step(i, carry):
        rows = pl.ds(pl.multiple_of(i * half, half), half)
        pre = mm(ra[0, pl.ds(2 * i, 2)].reshape(half, D), wu[...].reshape(D, FQ), 1, 0)
        sig = jax.nn.sigmoid(1.702 * pre)
        la[1, rows, :] = (pre * sig).astype(BF)
        gate[rows, :] = sig + 1.702 * pre * sig * (1.0 - sig)
        return carry

    lax.fori_loop(0, 2, up_step, 0)

    @pl.when(c == 0)
    def _():
        for k in range(NX):
            dl_copy(k).wait_recv()

    def cd_copy(p):
        return remote(gt.at[1, :, piece(p)], cr.at[:, piece(p)], "c", p, s + 1, d)

    def cu_copy(i):
        rows = slice(128 * i, 128 * i + 128)
        return remote(gt.at[0, rows], cr.at[rows], "c", i, s - 1, d)

    def down_in(p):
        cd_copy(p).wait_recv()
        xs[:, piece(p)] = (
            gt[1, :, piece(p)].astype(F32) + cr[:, piece(p)].astype(F32)
        ).astype(BF)

    def down_step(p):
        if p < NRELAY:
            for way in range(2):
                gf_copy(p, way).wait_recv()
        else:
            for k in range(1, NY):
                ga_copy(p, k).wait_recv()
        grads = ra[1, :, :, piece(p)].reshape(NY * TOK, PW)
        part = mm(grads, wd[:, :, piece(p)].reshape(FQ, PW), 1, 1)
        dact[...] = part if p == 0 else dact[...] + part
        gt[1, :, piece(p)] = mm(la[1], grads, 0, 0).astype(BF)

        @pl.when(c == 0)
        def _():
            cd_copy(p).start()

    def block(i):
        return pl.ds(pl.multiple_of(i * FF_DP, FF_DP), FF_DP)

    def xd_copy(p, k):
        to = (x + k) % NX
        return remote(
            xs.at[block(to), piece(p)], xr.at[x, :, piece(p)], "x", p * NX + k, s, x_peer(k)
        )

    def zd_copy(to, source):
        first = 128 * ((5 * to) // 4)
        return remote(
            zs.at[:, first : first + WIN], zr.at[source], "z", to, 2 * to + c, d, source
        )

    def down_out(p):
        down_in(p)
        for k in (2, 1, 3):
            xd_copy(p, k).start()

    def down_sum(p):
        for k in range(1, NX):
            xd_copy(p, k).wait_recv()
        xr[x, :, piece(p)] = xs[block(x), piece(p)]
        zs[:, piece(p)] = jnp.sum(xr[:, :, piece(p)].astype(F32), axis=0).astype(BF)
        for to in WHOLE[p]:

            @pl.when(z != to)
            def _(to=to):
                zd_copy(to, z).start()

            @pl.when(z == to)
            def _(to=to):
                first = 128 * ((5 * to) // 4)
                zr[to] = zs[:, first : first + WIN]

    def on_core_one(*steps):
        @pl.when(c == 1)
        def _():
            for step, p in steps:
                step(p)

    down_step(0)
    down_step(1)
    rows_in(3)
    on_core_one((down_out, 0), (down_out, 1))
    down_step(2)
    rows_in(4)
    on_core_one((down_out, 2), (down_sum, 0), (down_sum, 1))
    down_step(3)
    on_core_one((down_out, 3),)

    for k in range(1, NS):
        for p in range(NP):
            row_copy(p, k).wait_send()
        id_copy(k).wait_send()
    for k in range(1, ND):
        gain_copy(k).wait_send()

    down_step(4)
    la[0] = (dact[...] * gate[...]).astype(BF)
    on_core_one((down_out, 4),)

    def x_copy(r, k):
        to = (x + k) % NX
        rows = pl.ds(pl.multiple_of(to * FF_DP + r * RW, RW), RW)
        return remote(
            xs.at[rows], xr.at[x, pl.ds(r * RW, RW)], "x", r * NX + k, s, x_peer(k)
        )

    def norm_step(i, acc):
        rows = pl.ds(pl.multiple_of(i * half, half), half)
        part = mm(la[0, rows, :], wu[...].reshape(D, FQ), 1, 1)
        dns[pl.ds(2 * i, 2)] = part.astype(BF).reshape(2, TOK, D)
        normed = ra[0, pl.ds(2 * i, 2)].reshape(half, D).astype(F32)
        return acc + jnp.sum(part * normed, axis=0, keepdims=True)

    gp[...] = lax.fori_loop(0, 2, norm_step, jnp.zeros((1, D), F32))

    def dn_copy(k):
        to = (y + k) % NY
        return remote(dns.at[to], dnr.at[y], "dn", k, s, to * NX + x)

    for k in (2, 1, 3):
        dn_copy(k).start()

    def g1_copy(k):
        return remote(gp, gs1.at[s], "g1", k, (s + k) % NS, d)

    for k in range(1, NS):
        g1_copy(k).start()

    for i in range(FQ // 128):
        rows = slice(128 * i, 128 * i + 128)
        gt[0, rows, :] = mm(la[0, :, rows], ra[0].reshape(NY * TOK, D), 0, 0).astype(BF)

        @pl.when(c == 1)
        def _(i=i):
            cu_copy(i).start()

    on_core_one((down_sum, 2), (down_sum, 3), (down_sum, 4))

    def z_copy(r, k):
        to = (z + k) % NZ
        rows = pl.ds(r * RW, RW)
        return remote(
            zs.at[rows, pl.ds(window_start(to), WIN)],
            zr.at[z, rows],
            "z",
            r * NZ + k,
            2 * to + c,
            d,
        )

    @pl.when(c == 0)
    def _():
        for i in range(FQ // 128):
            cu_copy(i).wait_recv()
        for r in range(NR):
            for b in range(NX):
                rows = pl.ds(b * FF_DP + r * RW, RW)
                xs[rows, :] = (gt[0, rows, :].astype(F32) + cr[rows, :].astype(F32)).astype(BF)
            for k in (2, 1, 3):
                x_copy(r, k).start()
        for r in range(NR):
            rows = pl.ds(r * RW, RW)
            own = pl.ds(pl.multiple_of(x * FF_DP + r * RW, RW), RW)
            for k in range(1, NX):
                x_copy(r, k).wait_recv()
            xr[x, rows] = xs[own, :]
            zs[rows, :] = jnp.sum(xr[:, rows, :].astype(F32), axis=0).astype(BF)
            for k in (4, 3, 5, 2, 6, 1, 7):
                z_copy(r, k).start()
            zr[z, rows] = zs[rows, pl.ds(window_start(z), WIN)]

    gs1[s] = gp[...]
    for k in range(1, NS):
        g1_copy(k).wait_recv()
    gp2[...] = jnp.sum(gs1[...], axis=0)

    def g2_copy(k):
        return remote(gp2, gs2.at[d], "g2", k, s, (d + k) % ND)

    for k in range(1, ND):
        g2_copy(k).start()

    factor = 1.0 / math.sqrt(NS * ND * TOK)

    def window_sum():
        fs[...] = (jnp.sum(zr[...].astype(F32), axis=0) * factor).astype(BF)

    u_copy = remote(fs, fu, "f", 0, s + 1, d)
    d0_copy = remote(fs, fd, "f", 1, d, 2 * z)
    d1_copy = remote(fs, fd, "f", 2, d, 2 * z + 1, 1)
    own_down_out = pltpu.make_async_copy(fs, fd, s_loc.at[2])

    @pl.when(c == 1)
    def _():
        for source in range(NZ):

            @pl.when(z != source)
            def _(source=source):
                zd_copy(source, source).wait_recv()

        window_sum()
        d0_copy.start()

        @pl.when(s == d)
        def _():
            own_down_out.start()
            own_down_out.wait()

        @pl.when(s != d)
        def _():
            d1_copy.start()

    dnr[y] = dns[y]
    for k in range(1, NY):
        dn_copy(k).wait_recv()
    gain_again = jnp.sum(gr[...], axis=0)

    def resid_step(i, carry):
        rows = pl.ds(pl.multiple_of(i * 32, 32), 32)
        d_unit = jnp.sum(dnr[:, rows, :].astype(F32), axis=0) * gain_again
        normal = unit[rows, :]
        first = jnp.mean(d_unit, axis=1, keepdims=True)
        second = jnp.mean(d_unit * normal, axis=1, keepdims=True)
        d_hidden = inv[rows, :] * (d_unit - first - normal * second)
        gresid_ref[rows, :] = (ra[1, y, rows, :].astype(F32) + d_hidden).astype(BF)
        return carry

    lax.fori_loop(0, TOK // 32, resid_step, 0)

    stores[0].start()
    gq_tiles, gk_tiles, gv_tiles = Tiles(gq_ref), Tiles(gk_ref), Tiles(gv_ref)
    for h in range(HEADS):
        lanes, inside = window(h)
        grad = gresid_ref[:, lanes] * inside
        prob = probs[h]
        gv_tiles.add(h, mm(prob.astype(BF), grad, 0, 0))
        d_probs = mm(grad, v_ref[:, lanes], 1, 1)
        delta = jnp.sum(
            grad.astype(F32) * att[:, lanes].astype(F32), axis=1, keepdims=True
        )
        d_scores = (prob * (d_probs - delta) * scale).astype(BF)
        gq_tiles.add(h, mm(d_scores, k_ref[:, lanes] * inside, 1, 0))
        gk_tiles.add(h, mm(d_scores, q_ref[:, lanes] * inside, 0, 0))
    for copy in stores[1:]:
        copy.start()

    gs2[d] = gp2[...]
    for k in range(1, ND):
        g2_copy(k).wait_recv()
    ggain_ref[...] = jnp.sum(gs2[...], axis=0) * factor / gain_again

    def chosen(first):
        return jnp.where(
            iota((ROWS_DP, WIN), 1) == iota((ROWS_DP, WIN), 0) + first, 1.0, 0.0
        ).astype(BF)

    own_lanes = chosen(32 * (z % 4) + ROWS_DP * c)

    @pl.when(c == 0)
    def _():
        for r in range(NR):
            for k in range(1, NZ):
                z_copy(r, k).wait_recv()
        window_sum()
        u_copy.start()
        up_ref[...] = mm(own_lanes, fs[...], 1, 1).astype(BF)

    @pl.when(c == 1)
    def _():
        u_copy.wait_recv()
        up_ref[...] = mm(own_lanes, fu[...], 1, 1).astype(BF)

    @pl.when(jnp.logical_not(own_final))
    def _():
        d0_copy.wait_recv()

    down_ref[...] = mm(
        fd[...], chosen(32 * ((d // 2) % 4) + ROWS_DP * (d % 2)), 1, 1
    ).astype(BF)

    @pl.when(c == 0)
    def _():
        u_copy.wait_send()
        for k in range(1, NY):
            wy_copy(k).wait_send()
        for k in range(1, NX):
            ux_copy(k).wait_send()
        for k in range(NX):
            ul_copy(k).wait_send()
        for p in range(NP):
            cd_copy(p).wait_send()
        for r in range(NR):
            for k in range(1, NX):
                x_copy(r, k).wait_send()
            for k in range(1, NZ):
                z_copy(r, k).wait_send()

    @pl.when(c == 1)
    def _():
        d0_copy.wait_send()

        @pl.when(s != d)
        def _():
            d1_copy.wait_send()

        for k in range(1, NX):
            dx_copy(k).wait_send()
        for k in range(NX):
            dl_copy(k).wait_send()
        for i in range(FQ // 128):
            cu_copy(i).wait_send()
        for p in range(NP):
            for k in range(1, NX):
                xd_copy(p, k).wait_send()
        for to in range(NZ):

            @pl.when(z != to)
            def _(to=to):
                zd_copy(to, z).wait_send()

    for k in range(1, NS):
        g1_copy(k).wait_send()
    for k in range(1, ND):
        g2_copy(k).wait_send()
    for k in range(1, NY):
        if k != 2:
            na_copy(k).wait_send()
        for p in range(NP):
            if k != 2 or p >= NRELAY:
                ga_copy(p, k).wait_send()
        dn_copy(k).wait_send()
    for way in range(2):
        nf_copy(way).wait_send()
        for p in range(NRELAY):
            gf_copy(p, way).wait_send()
    for copy in stores:
        copy.wait()


def layer(*args):
    vm = pl.BlockSpec(memory_space=pltpu.VMEM)
    hbm = pl.BlockSpec(memory_space=pl.ANY)
    sem = pltpu.SemaphoreType.DMA
    sems = [sem((12,))]
    for n in SEMS.values():
        sems += [sem((n,)), sem((n,))]
    out = jax.ShapeDtypeStruct
    return pl.pallas_call(
        kernel,
        out_shape=(
            out((TOK, D), BF),
            out((TOK, D), BF),
            out((TOK, D), BF),
            out((TOK, D), BF),
            out((ROWS_DP, FF_DP), BF),
            out((FF_DP, ROWS_DP), BF),
            out((1, D), F32),
        ),
        in_specs=[hbm] * 5 + [vm, vm, hbm, hbm, vm],
        out_specs=(hbm,) * 4 + (vm,) * 3,
        scratch_shapes=[
            *[pltpu.VMEM((TOK, D), BF)] * 4,
            pltpu.VMEM((POS, D), BF),
            *[pltpu.VMEM((TOK, D), BF)] * 4,
            pltpu.VMEM((NP, NS, CAP, PW), BF),
            pltpu.VMEM((NP, NS, CAP, PW), BF),
            pltpu.VMEM((NS, 1, 128), F32),
            pltpu.VMEM((NS, 1, 128), F32),
            pltpu.VMEM((1, D), F32),
            pltpu.VMEM((ND, 1, D), F32),
            pltpu.VMEM((NY, NX, ROWS_DP, FQ), BF),
            pltpu.VMEM((NX, FF_DP, D), BF),
            pltpu.VMEM((2, NY, TOK, D), BF),
            pltpu.VMEM((2, NY * TOK, FQ), BF),
            pltpu.VMEM((NY * TOK, FQ), F32),
            pltpu.VMEM((NY * TOK, FQ), F32),
            pltpu.VMEM((NY, TOK, D), BF),
            pltpu.VMEM((NY, TOK, D), BF),
            pltpu.VMEM((2, FQ, D), BF),
            pltpu.VMEM((FQ, D), BF),
            pltpu.VMEM((FQ, D), BF),
            pltpu.VMEM((NX, FF_DP, D), BF),
            pltpu.VMEM((FF_DP, D), BF),
            pltpu.VMEM((NZ, FF_DP, WIN), BF),
            pltpu.VMEM((FF_DP, WIN), BF),
            pltpu.VMEM((FF_DP, WIN), BF),
            pltpu.VMEM((FF_DP, WIN), BF),
            pltpu.VMEM((1, D), F32),
            pltpu.VMEM((NS, 1, D), F32),
            pltpu.VMEM((1, D), F32),
            pltpu.VMEM((ND, 1, D), F32),
            pltpu.VMEM((HEADS, TOK, TOK), F32),
            pltpu.VMEM((TOK, D), BF),
            pltpu.VMEM((TOK, D), F32),
            pltpu.VMEM((TOK, 1), F32),
            *sems,
        ],
        compiler_params=pltpu.CompilerParams(
            collective_id=0, has_side_effects=True, vmem_limit_bytes=56 * 2**20
        ),
    )(*args)


def hand_out_kernel(*refs):
    n = 7
    ins, outs, held, taken, done = refs[:n], refs[n : 2 * n], refs[2 * n : -2], refs[-2], refs[-1]
    into = [pltpu.make_async_copy(ins[i], held[i], taken.at[i]) for i in range(4)]
    out = [
        pltpu.make_async_copy(held[i] if i < 4 else ins[i], outs[i], done.at[i])
        for i in range(n - 1)
    ]
    for copy in into:
        copy.start()
    for copy in out[4:]:
        copy.start()
    outs[n - 1][...] = ins[n - 1][0, :]
    for i in range(4):
        into[i].wait()
        out[i].start()
    for copy in out:
        copy.wait()


def hand_out(arrays):
    vm = pl.BlockSpec(memory_space=pltpu.VMEM)
    hbm = pl.BlockSpec(memory_space=pl.ANY)
    return pl.pallas_call(
        hand_out_kernel,
        out_shape=tuple(jax.ShapeDtypeStruct(a.shape, a.dtype) for a in arrays[:-1])
        + (jax.ShapeDtypeStruct((D,), F32),),
        in_specs=[hbm] * 4 + [vm] * 3,
        out_specs=(hbm,) * 6 + (vm,),
        scratch_shapes=[
            *[pltpu.VMEM((TOK, D), BF)] * 4,
            pltpu.SemaphoreType.DMA((4,)),
            pltpu.SemaphoreType.DMA((6,)),
        ],
    )(*arrays)


def per_device(
    queries, key_rows, value_rows, resid_in, llm_grad, vision_slot, window_mask, w_up, w_down,
    norm_gain,
):
    results = layer(
        queries[0],
        key_rows[0],
        value_rows[0],
        resid_in[0],
        llm_grad[0],
        vision_slot,
        window_mask,
        w_up,
        w_down,
        norm_gain.reshape(1, ROWS_DP),
    )
    grad_query, grad_key, grad_value, grad_resid, grad_up, grad_down, grad_gain = hand_out(results)
    return (
        grad_query[None],
        grad_key[None],
        grad_value[None],
        grad_resid[None],
        grad_up,
        grad_down,
        grad_gain,
    )


def solution(mesh):
    row3 = P("dp", "seq", None)
    in_specs = (
        row3,
        row3,
        row3,
        row3,
        row3,
        P("dp", "seq"),
        row3,
        P("dp", None),
        P("dp", None),
        P("dp"),
    )
    out_specs = (row3, row3, row3, row3, P("seq", "dp"), P("seq", "dp"), P())
    return jax.shard_map(
        per_device, mesh=mesh, in_specs=in_specs, out_specs=out_specs, check_vma=False
    )
```

```python
import math

import jax
import jax.numpy as jnp
from jax import lax
from jax.experimental import pallas as pl
from jax.experimental.pallas import tpu as pltpu
from jax.sharding import PartitionSpec as P

HEADS = 16
HDIM = 80
BLK = 64
D = 1280
FF = 2560
TOK = 128
POS = 192
NS = 16
ND = 16
CAP = 32
NY, NX, NZ = 4, 4, 8
FQ = FF // NY
ROWS_DP = D // ND
FF_DP = FF // ND
WIN = 256
NP = 5
PW = D // NP
NRELAY = 3
NR = 5
RW = FF_DP // NR
WHOLE = ((0,), (1, 2), (3,), (4, 5), (6, 7))
MESH = pl.DeviceIdType.MESH
BF = jnp.bfloat16
F32 = jnp.float32


def mm(left, right, left_dim, right_dim):
    return lax.dot_general(
        left, right, (((left_dim,), (right_dim,)), ((), ())), preferred_element_type=F32
    )


def iota(shape, dim):
    return lax.broadcasted_iota(jnp.int32, shape, dim)


def to_column(row):
    n = row.shape[1]
    same = iota((n, n), 0) == iota((n, n), 1)
    return jnp.sum(jnp.where(same, row, 0.0), axis=1, keepdims=True)


def window_start(z):
    return pl.multiple_of(128 * ((5 * z) // 4), 128)


SEMS = {
    "gr": ND, "rr": NP * NS, "ri": NS, "wy": NY, "wx": NX, "rl": NX, "na": NY, "nf": 2, "ga": NP * NY, "gf": NP * 2,
    "dn": NY, "c": 5, "x": NR * NX, "z": NR * NZ, "f": 3, "g1": NS, "g2": ND,
}


def kernel(
    q_hbm, k_hbm, v_hbm, resid_hbm, llm_hbm, slot_hbm, mask_hbm, wup_ref, wdown_ref, ngain_hbm,
    gq_hbm, gk_hbm, gv_hbm, gresid_hbm, up_hbm, down_hbm, ggain_hbm,
    slot_ref, mask_ref, ngain_ref, up_ref, down_ref, ggain_ref,
    q_ref, k_ref, v_ref, resid_ref, llm_ref, gq_ref, gk_ref, gv_ref, gresid_ref,
    rs, rr, ids, ri, gsh, gr, wu, wd, ra, la, gate, dact, dns, dnr, gt, cr, xs, xr, zs, zr,
    fs, fu, fd, gp, gs1, gp2, gs2, probs, att, unit, inv, s_loc, *sems,
):
    names = list(SEMS)
    send = {n: sems[2 * i] for i, n in enumerate(names)}
    recv = {n: sems[2 * i + 1] for i, n in enumerate(names)}
    s = lax.axis_index("seq")
    d = lax.axis_index("dp")
    z, c = s // 2, s % 2
    y, x = d // NX, d % NX
    scale = 1.0 / math.sqrt(HDIM)

    def remote(src, dst, name, at, to_s, to_d, at_recv=None):
        return pltpu.make_async_remote_copy(
            src_ref=src,
            dst_ref=dst,
            send_sem=send[name].at[at],
            recv_sem=recv[name].at[at if at_recv is None else at_recv],
            device_id=(to_s, to_d),
            device_id_type=MESH,
        )

    def y_peer(k):
        return ((y + k) % NY) * NX + x

    def x_peer(k):
        return y * NX + (x + k) % NX

    def local(src, dst, at):
        return pltpu.make_async_copy(src, dst, s_loc.at[at])

    small = [
        local(slot_hbm, slot_ref, 12),
        local(ngain_hbm, ngain_ref, 13),
        local(mask_hbm, mask_ref, 14),
    ]
    for copy in small:
        copy.start()
    loads = [
        local(llm_hbm, llm_ref, 3),
        local(q_hbm, q_ref, 4),
        local(k_hbm, k_ref, 5),
        local(v_hbm, v_ref, 6),
        local(resid_hbm, resid_ref, 7),
    ]
    stores = [
        local(gresid_ref, gresid_hbm, 8),
        local(gq_ref, gq_hbm, 9),
        local(gk_ref, gk_hbm, 10),
        local(gv_ref, gv_hbm, 11),
    ]
    for copy in loads:
        copy.start()

    barrier = pltpu.get_barrier_semaphore()
    for k in range(1, NS):
        pl.semaphore_signal(barrier, inc=1, device_id=((s + k) % NS, d), device_id_type=MESH)
    for k in range(1, ND):
        pl.semaphore_signal(barrier, inc=1, device_id=(s, (d + k) % ND), device_id_type=MESH)
    from_s = 2 * (d // 2) + 1
    own_final = jnp.logical_and(from_s == s, s == d)

    @pl.when(jnp.logical_not(own_final))
    def _():
        pl.semaphore_signal(barrier, inc=1, device_id=(from_s, s), device_id_type=MESH)

    for copy in small:
        copy.wait()
    slot_row = slot_ref[...].astype(F32)
    slot_col = to_column(slot_row)
    owner_row = jnp.floor(slot_row * (1.0 / TOK))
    owner_col = jnp.floor(slot_col * (1.0 / TOK))
    at0, at1 = iota((POS, POS), 0), iota((POS, POS), 1)
    same = owner_col == owner_row
    rank_row = jnp.sum(jnp.where(same & (at0 < at1), 1.0, 0.0), axis=0, keepdims=True)
    rank_col = jnp.sum(jnp.where(same & (at1 < at0), 1.0, 0.0), axis=1, keepdims=True)
    target_row = jnp.where(slot_row >= 0.0, owner_row * CAP + rank_row, -1.0)
    target_col = jnp.where(slot_col >= 0.0, owner_col * CAP + rank_col, -1.0)
    hit = iota((NS * CAP, POS), 0).astype(F32) == target_row
    pick = jnp.where(hit, 1.0, 0.0).astype(BF)

    def pack(p):
        rs[p] = mm(pick, llm_ref[:, PW * p : PW * p + PW], 1, 0).astype(BF).reshape(NS, CAP, PW)

    loads[0].wait()
    pack(0)
    pl.semaphore_wait(barrier, NS + ND - 2 + 2 * c - jnp.where(own_final, 1, 0))

    def gain_copy(k):
        return remote(gsh, gr.at[d], "gr", k, s, (d + k) % ND)

    def row_copy(p, k):
        to = (s + k) % NS
        return remote(rs.at[p, to], rr.at[p, s], "rr", p * NS + k, to, d)

    def id_copy(k):
        to = (s + k) % NS
        return remote(ids.at[to], ri.at[s], "ri", k, to, d)

    far_first = (8, 7, 9, 6, 10, 5, 11, 4, 12, 3, 13, 2, 14, 1, 15)
    for k in far_first:
        row_copy(0, k).start()

    def quarter(q):
        return wup_ref.at[:, pl.ds(pl.multiple_of(q * FQ, 128), FQ)]

    def wy_copy(k):
        return remote(quarter((y + k) % NY), wu.at[y, x], "wy", k, s, y_peer(k))

    def ux_copy(k):
        return remote(wu.at[:, x], wu.at[:, x], "wx", k, s, x_peer(k))

    def dx_copy(k):
        return remote(wd.at[x], wd.at[x], "wx", k, s, x_peer(k))

    def ul_copy(k):
        at = (x + NX - k) % NX
        return remote(wu.at[:, at], wu.at[:, at], "rl", k, s + 1, d)

    def dl_copy(k):
        at = (x + NX - k) % NX
        return remote(wd.at[at], wd.at[at], "rl", k, s - 1, d)

    own_up = pltpu.make_async_copy(quarter(y), wu.at[y, x], s_loc.at[0])
    own_down = pltpu.make_async_copy(wdown_ref, wd.at[x], s_loc.at[1])

    @pl.when(c == 0)
    def _():
        for k in (2, 1, 3):
            wy_copy(k).start()
        own_up.start()
        own_up.wait()

    @pl.when(c == 1)
    def _():
        own_down.start()
        own_down.wait()
        for k in (2, 1, 3):
            dx_copy(k).start()
        dl_copy(0).start()

    lane = iota((1, 128), 1)
    lane_slot = (lane % CAP).astype(F32)
    mine = lane // CAP == s % 4
    landing = slot_col - owner_col * TOK + 1.0
    for o in range(NS):
        found = jnp.where((target_col == lane_slot + float(o * CAP)) & mine, landing, 0.0)
        ids[o] = jnp.sum(found, axis=0, keepdims=True) - 1.0
    ngain_col = to_column(ngain_ref[...].astype(F32))
    place_gain = iota((ROWS_DP, D), 1) == iota((ROWS_DP, D), 0) + d * ROWS_DP
    gsh[...] = jnp.sum(jnp.where(place_gain, ngain_col, 0.0), axis=0, keepdims=True)

    for k in far_first:
        id_copy(k).start()
    for k in range(1, ND):
        gain_copy(k).start()
    for p in range(1, NP):
        pack(p)
        for k in far_first:
            row_copy(p, k).start()
    for p in range(NP):
        rr[p, s] = rs[p, s]
    ri[s] = ids[s]

    row_late = iota((TOK, TOK), 0) >= BLK
    col_late = iota((TOK, TOK), 1) >= BLK
    flags = [[mask_ref[0, i : i + 1, j : j + 1] for j in range(2)] for i in range(2)]
    allowed = (
        jnp.where(
            row_late,
            jnp.where(col_late, flags[1][1], flags[1][0]),
            jnp.where(col_late, flags[0][1], flags[0][0]),
        )
        > 0
    )

    def window(h):
        first, last = HDIM * h // 128, (HDIM * h + HDIM - 1) // 128
        lanes = slice(128 * first, 128 * last + 128)
        feature = iota((1, lanes.stop - lanes.start), 1) + lanes.start
        inside = (feature >= HDIM * h) & (feature < HDIM * h + HDIM)
        return lanes, jnp.where(inside, 1.0, 0.0).astype(BF)

    class Tiles:
        def __init__(self, out):
            self.out, self.open = out, {}

        def add(self, h, value):
            first = HDIM * h // 128
            for i in range(value.shape[1] // 128):
                part = value[:, 128 * i : 128 * i + 128]
                held = self.open.get(first + i)
                self.open[first + i] = part if held is None else held + part
            upto = HDIM * (h + 1) // 128 if h + 1 < HEADS else D // 128
            for t in [t for t in self.open if t < upto]:
                self.out[:, 128 * t : 128 * t + 128] = self.open.pop(t).astype(BF)

    att_tiles = Tiles(att)

    def attend(h):
        lanes, inside = window(h)
        scores = mm(q_ref[:, lanes], k_ref[:, lanes] * inside, 1, 1) * scale
        masked = jnp.where(allowed, scores, -jnp.inf)
        highest = jnp.max(masked, axis=1, keepdims=True)
        terms = jnp.where(allowed, jnp.exp(masked - highest), 0.0)
        prob = terms * (1.0 / jnp.sum(terms, axis=1, keepdims=True))
        probs[h] = prob
        att_tiles.add(h, mm(prob.astype(BF), v_ref[:, lanes] * inside, 1, 0))

    for copy in loads[1:]:
        copy.wait()
    for h in range(HEADS // 2):
        attend(h)

    @pl.when(c == 0)
    def _():
        for k in range(1, NY):
            wy_copy(k).wait_recv()
        for k in (2, 1, 3):
            ux_copy(k).start()
        ul_copy(0).start()

    for h in range(HEADS // 2, HEADS):
        attend(h)

    gr[d] = gsh[...]
    for k in range(1, ND):
        gain_copy(k).wait_recv()
    gain_full = jnp.sum(gr[...], axis=0)

    def unit_step(i, carry):
        rows = pl.ds(pl.multiple_of(i * 32, 32), 32)
        hidden = resid_ref[rows, :].astype(F32) + att[rows, :].astype(F32)
        center = jnp.mean(hidden, axis=1, keepdims=True)
        away = hidden - center
        inverse = lax.rsqrt(jnp.mean(away * away, axis=1, keepdims=True) + 1e-06)
        inv[rows, :] = inverse
        out = away * inverse
        unit[rows, :] = out
        ra[0, y, rows, :] = (out * gain_full).astype(BF)
        return carry

    lax.fori_loop(0, TOK // 32, unit_step, 0)

    def na_copy(k):
        return remote(ra.at[0, y], ra.at[0, y], "na", k, s, y_peer(k))

    for k in (1, 3):
        na_copy(k).start()

    def nf_copy(way):
        at = (y + NY - 1) % NY if way == 0 else (y + 1) % NY
        view = ra.at[0, at, pl.ds(way * BLK, BLK)]
        return remote(view, view, "nf", way, s, y_peer(1 if way == 0 else 3))

    def n_forward():
        for way, k in ((0, 1), (1, 3)):
            na_copy(k).wait_recv()
            nf_copy(way).start()

    @pl.when(c == 1)
    def _():
        for k in (1, 3, 2):
            dx_copy(k).wait_recv()
            dl_copy(k).start()

    for k in range(1, NS):
        id_copy(k).wait_recv()
    token = iota((TOK, 128), 0).astype(F32)
    place = jnp.concatenate(
        [
            jnp.where(token == jnp.max(ri[4 * j : 4 * j + 4], axis=0), 1.0, 0.0).astype(BF)
            for j in range(4)
        ],
        axis=1,
    )

    def piece(p):
        return slice(PW * p, PW * p + PW)

    def ga_copy(p, k):
        view = ra.at[1, y, :, piece(p)]
        return remote(view, view, "ga", p * NY + k, s, y_peer(k))

    def gf_copy(p, way):
        at = (y + NY - 1) % NY if way == 0 else (y + 1) % NY
        view = ra.at[1, at, pl.ds(way * BLK, BLK), piece(p)]
        return remote(view, view, "gf", p * 2 + way, s, y_peer(1 if way == 0 else 3))

    def rows_in(p):
        for k in range(1, NS):
            row_copy(p, k).wait_recv()
        ra[1, y, :, piece(p)] = mm(place, rr[p].reshape(NS * CAP, PW), 1, 0).astype(BF)
        for k in (1, 3) if p < NRELAY else (2, 1, 3):
            ga_copy(p, k).start()
        if 0 < p <= NRELAY:
            for way, k in ((0, 1), (1, 3)):
                ga_copy(p - 1, k).wait_recv()
                gf_copy(p - 1, way).start()

    rows_in(0)
    rows_in(1)
    n_forward()
    rows_in(2)

    @pl.when(c == 0)
    def _():
        for k in (1, 3, 2):
            ux_copy(k).wait_recv()
            ul_copy(k).start()

    @pl.when(c == 1)
    def _():
        for k in range(NX):
            ul_copy(k).wait_recv()

    for way in range(2):
        nf_copy(way).wait_recv()
    half = 2 * TOK

    def up_step(i, carry):
        rows = pl.ds(pl.multiple_of(i * half, half), half)
        pre = mm(ra[0, pl.ds(2 * i, 2)].reshape(half, D), wu[...].reshape(D, FQ), 1, 0)
        sig = jax.nn.sigmoid(1.702 * pre)
        la[1, rows, :] = (pre * sig).astype(BF)
        gate[rows, :] = sig + 1.702 * pre * sig * (1.0 - sig)
        return carry

    lax.fori_loop(0, 2, up_step, 0)

    @pl.when(c == 0)
    def _():
        for k in range(NX):
            dl_copy(k).wait_recv()

    def cd_copy(p):
        return remote(gt.at[1, :, piece(p)], cr.at[:, piece(p)], "c", p, s + 1, d)

    def cu_copy(i):
        rows = slice(128 * i, 128 * i + 128)
        return remote(gt.at[0, rows], cr.at[rows], "c", i, s - 1, d)

    def down_in(p):
        cd_copy(p).wait_recv()
        xs[:, piece(p)] = (
            gt[1, :, piece(p)].astype(F32) + cr[:, piece(p)].astype(F32)
        ).astype(BF)

    def down_step(p):
        if p < NRELAY:
            for way in range(2):
                gf_copy(p, way).wait_recv()
        else:
            for k in range(1, NY):
                ga_copy(p, k).wait_recv()
        grads = ra[1, :, :, piece(p)].reshape(NY * TOK, PW)
        part = mm(grads, wd[:, :, piece(p)].reshape(FQ, PW), 1, 1)
        dact[...] = part if p == 0 else dact[...] + part
        gt[1, :, piece(p)] = mm(la[1], grads, 0, 0).astype(BF)

        @pl.when(c == 0)
        def _():
            cd_copy(p).start()

    def block(i):
        return pl.ds(pl.multiple_of(i * FF_DP, FF_DP), FF_DP)

    def xd_copy(p, k):
        to = (x + k) % NX
        return remote(
            xs.at[block(to), piece(p)], xr.at[x, :, piece(p)], "x", p * NX + k, s, x_peer(k)
        )

    def zd_copy(to, source):
        first = 128 * ((5 * to) // 4)
        return remote(
            zs.at[:, first : first + WIN], zr.at[source], "z", to, 2 * to + c, d, source
        )

    def down_out(p):
        down_in(p)
        for k in (2, 1, 3):
            xd_copy(p, k).start()

    def down_sum(p):
        for k in range(1, NX):
            xd_copy(p, k).wait_recv()
        xr[x, :, piece(p)] = xs[block(x), piece(p)]
        zs[:, piece(p)] = jnp.sum(xr[:, :, piece(p)].astype(F32), axis=0).astype(BF)
        for to in WHOLE[p]:

            @pl.when(z != to)
            def _(to=to):
                zd_copy(to, z).start()

            @pl.when(z == to)
            def _(to=to):
                first = 128 * ((5 * to) // 4)
                zr[to] = zs[:, first : first + WIN]

    def on_core_one(*steps):
        @pl.when(c == 1)
        def _():
            for step, p in steps:
                step(p)

    down_step(0)
    down_step(1)
    rows_in(3)
    on_core_one((down_out, 0), (down_out, 1))
    down_step(2)
    rows_in(4)
    on_core_one((down_out, 2),)
    down_step(3)

    for k in range(1, NS):
        for p in range(NP):
            row_copy(p, k).wait_send()
        id_copy(k).wait_send()
    for k in range(1, ND):
        gain_copy(k).wait_send()

    down_step(4)
    la[0] = (dact[...] * gate[...]).astype(BF)

    def x_copy(r, k):
        to = (x + k) % NX
        rows = pl.ds(pl.multiple_of(to * FF_DP + r * RW, RW), RW)
        return remote(
            xs.at[rows], xr.at[x, pl.ds(r * RW, RW)], "x", r * NX + k, s, x_peer(k)
        )

    def norm_step(i, acc):
        rows = pl.ds(pl.multiple_of(i * half, half), half)
        part = mm(la[0, rows, :], wu[...].reshape(D, FQ), 1, 1)
        dns[pl.ds(2 * i, 2)] = part.astype(BF).reshape(2, TOK, D)
        normed = ra[0, pl.ds(2 * i, 2)].reshape(half, D).astype(F32)
        return acc + jnp.sum(part * normed, axis=0, keepdims=True)

    gp[...] = lax.fori_loop(0, 2, norm_step, jnp.zeros((1, D), F32))

    def dn_copy(k):
        to = (y + k) % NY
        return remote(dns.at[to], dnr.at[y], "dn", k, s, to * NX + x)

    for k in (2, 1, 3):
        dn_copy(k).start()

    def g1_copy(k):
        return remote(gp, gs1.at[s], "g1", k, (s + k) % NS, d)

    for k in range(1, NS):
        g1_copy(k).start()

    for i in range(FQ // 128):
        rows = slice(128 * i, 128 * i + 128)
        gt[0, rows, :] = mm(la[0, :, rows], ra[0].reshape(NY * TOK, D), 0, 0).astype(BF)

        @pl.when(c == 1)
        def _(i=i):
            cu_copy(i).start()

    on_core_one(
        (down_out, 3),
        (down_out, 4),
        (down_sum, 0),
        (down_sum, 1),
        (down_sum, 2),
        (down_sum, 3),
        (down_sum, 4),
    )

    def z_copy(r, k):
        to = (z + k) % NZ
        rows = pl.ds(r * RW, RW)
        return remote(
            zs.at[rows, pl.ds(window_start(to), WIN)],
            zr.at[z, rows],
            "z",
            r * NZ + k,
            2 * to + c,
            d,
        )

    @pl.when(c == 0)
    def _():
        for i in range(FQ // 128):
            cu_copy(i).wait_recv()
        for r in range(NR):
            for b in range(NX):
                rows = pl.ds(b * FF_DP + r * RW, RW)
                xs[rows, :] = (gt[0, rows, :].astype(F32) + cr[rows, :].astype(F32)).astype(BF)
            for k in (2, 1, 3):
                x_copy(r, k).start()
        for r in range(NR):
            rows = pl.ds(r * RW, RW)
            own = pl.ds(pl.multiple_of(x * FF_DP + r * RW, RW), RW)
            for k in range(1, NX):
                x_copy(r, k).wait_recv()
            xr[x, rows] = xs[own, :]
            zs[rows, :] = jnp.sum(xr[:, rows, :].astype(F32), axis=0).astype(BF)
            for k in (4, 3, 5, 2, 6, 1, 7):
                z_copy(r, k).start()
            zr[z, rows] = zs[rows, pl.ds(window_start(z), WIN)]

    gs1[s] = gp[...]
    for k in range(1, NS):
        g1_copy(k).wait_recv()
    gp2[...] = jnp.sum(gs1[...], axis=0)

    def g2_copy(k):
        return remote(gp2, gs2.at[d], "g2", k, s, (d + k) % ND)

    for k in range(1, ND):
        g2_copy(k).start()

    factor = 1.0 / math.sqrt(NS * ND * TOK)

    def window_sum():
        fs[...] = (jnp.sum(zr[...].astype(F32), axis=0) * factor).astype(BF)

    u_copy = remote(fs, fu, "f", 0, s + 1, d)
    d0_copy = remote(fs, fd, "f", 1, d, 2 * z)
    d1_copy = remote(fs, fd, "f", 2, d, 2 * z + 1, 1)
    own_down_out = pltpu.make_async_copy(fs, fd, s_loc.at[2])

    @pl.when(c == 1)
    def _():
        for source in range(NZ):

            @pl.when(z != source)
            def _(source=source):
                zd_copy(source, source).wait_recv()

        window_sum()
        d0_copy.start()

        @pl.when(s == d)
        def _():
            own_down_out.start()
            own_down_out.wait()

        @pl.when(s != d)
        def _():
            d1_copy.start()

    dnr[y] = dns[y]
    for k in range(1, NY):
        dn_copy(k).wait_recv()
    gain_again = jnp.sum(gr[...], axis=0)

    def resid_step(i, carry):
        rows = pl.ds(pl.multiple_of(i * 32, 32), 32)
        d_unit = jnp.sum(dnr[:, rows, :].astype(F32), axis=0) * gain_again
        normal = unit[rows, :]
        first = jnp.mean(d_unit, axis=1, keepdims=True)
        second = jnp.mean(d_unit * normal, axis=1, keepdims=True)
        d_hidden = inv[rows, :] * (d_unit - first - normal * second)
        gresid_ref[rows, :] = (ra[1, y, rows, :].astype(F32) + d_hidden).astype(BF)
        return carry

    lax.fori_loop(0, TOK // 32, resid_step, 0)

    def chosen(first):
        return jnp.where(
            iota((ROWS_DP, WIN), 1) == iota((ROWS_DP, WIN), 0) + first, 1.0, 0.0
        ).astype(BF)

    own_lanes = chosen(32 * (z % 4) + ROWS_DP * c)

    def gain_end():
        gs2[d] = gp2[...]
        for k in range(1, ND):
            g2_copy(k).wait_recv()
        ggain_ref[...] = jnp.sum(gs2[...], axis=0) * factor / gain_again
        local(ggain_ref, ggain_hbm, 17).start()

    def up_end():
        @pl.when(c == 0)
        def _():
            for r in range(NR):
                for k in range(1, NZ):
                    z_copy(r, k).wait_recv()
            window_sum()
            u_copy.start()
            up_ref[...] = mm(own_lanes, fs[...], 1, 1).astype(BF)

    def outputs_end():
        @pl.when(c == 1)
        def _():
            u_copy.wait_recv()
            up_ref[...] = mm(own_lanes, fu[...], 1, 1).astype(BF)

        @pl.when(jnp.logical_not(own_final))
        def _():
            d0_copy.wait_recv()

        down_ref[...] = mm(
            fd[...], chosen(32 * ((d // 2) % 4) + ROWS_DP * (d % 2)), 1, 1
        ).astype(BF)
        local(up_ref, up_hbm, 15).start()
        local(down_ref, down_hbm, 16).start()

    stores[0].start()
    gq_tiles, gk_tiles, gv_tiles = Tiles(gq_ref), Tiles(gk_ref), Tiles(gv_ref)
    for h in range(HEADS):
        lanes, inside = window(h)
        grad = gresid_ref[:, lanes] * inside
        prob = probs[h]
        gv_tiles.add(h, mm(prob.astype(BF), grad, 0, 0))
        d_probs = mm(grad, v_ref[:, lanes], 1, 1)
        delta = jnp.sum(
            grad.astype(F32) * att[:, lanes].astype(F32), axis=1, keepdims=True
        )
        d_scores = (prob * (d_probs - delta) * scale).astype(BF)
        gq_tiles.add(h, mm(d_scores, k_ref[:, lanes] * inside, 1, 0))
        gk_tiles.add(h, mm(d_scores, q_ref[:, lanes] * inside, 0, 0))
        if h == 7:
            up_end()
        elif h == 11:
            outputs_end()
            gain_end()
    for copy in stores[1:]:
        copy.start()

    @pl.when(c == 0)
    def _():
        u_copy.wait_send()
        for k in range(1, NY):
            wy_copy(k).wait_send()
        for k in range(1, NX):
            ux_copy(k).wait_send()
        for k in range(NX):
            ul_copy(k).wait_send()
        for p in range(NP):
            cd_copy(p).wait_send()
        for r in range(NR):
            for k in range(1, NX):
                x_copy(r, k).wait_send()
            for k in range(1, NZ):
                z_copy(r, k).wait_send()

    @pl.when(c == 1)
    def _():
        d0_copy.wait_send()

        @pl.when(s != d)
        def _():
            d1_copy.wait_send()

        for k in range(1, NX):
            dx_copy(k).wait_send()
        for k in range(NX):
            dl_copy(k).wait_send()
        for i in range(FQ // 128):
            cu_copy(i).wait_send()
        for p in range(NP):
            for k in range(1, NX):
                xd_copy(p, k).wait_send()
        for to in range(NZ):

            @pl.when(z != to)
            def _(to=to):
                zd_copy(to, z).wait_send()

    for k in range(1, NS):
        g1_copy(k).wait_send()
    for k in range(1, ND):
        g2_copy(k).wait_send()
    for k in range(1, NY):
        if k != 2:
            na_copy(k).wait_send()
        for p in range(NP):
            if k != 2 or p >= NRELAY:
                ga_copy(p, k).wait_send()
        dn_copy(k).wait_send()
    for way in range(2):
        nf_copy(way).wait_send()
        for p in range(NRELAY):
            gf_copy(p, way).wait_send()
    for copy in stores:
        copy.wait()
    local(up_ref, up_hbm, 15).wait()
    local(down_ref, down_hbm, 16).wait()
    local(ggain_ref, ggain_hbm, 17).wait()


def layer(*args):
    hbm = pl.BlockSpec(memory_space=pl.ANY)
    sem = pltpu.SemaphoreType.DMA
    sems = [sem((20,))]
    for n in SEMS.values():
        sems += [sem((n,)), sem((n,))]
    out = jax.ShapeDtypeStruct
    return pl.pallas_call(
        kernel,
        out_shape=(
            out((TOK, D), BF),
            out((TOK, D), BF),
            out((TOK, D), BF),
            out((TOK, D), BF),
            out((ROWS_DP, FF_DP), BF),
            out((FF_DP, ROWS_DP), BF),
            out((1, D), F32),
        ),
        in_specs=[hbm] * 10,
        out_specs=(hbm,) * 7,
        scratch_shapes=[
            pltpu.VMEM((1, POS), jnp.int32),
            pltpu.VMEM((1, 2, 2), jnp.int32),
            pltpu.VMEM((1, ROWS_DP), BF),
            pltpu.VMEM((ROWS_DP, FF_DP), BF),
            pltpu.VMEM((FF_DP, ROWS_DP), BF),
            pltpu.VMEM((1, D), F32),
            *[pltpu.VMEM((TOK, D), BF)] * 4,
            pltpu.VMEM((POS, D), BF),
            *[pltpu.VMEM((TOK, D), BF)] * 4,
            pltpu.VMEM((NP, NS, CAP, PW), BF),
            pltpu.VMEM((NP, NS, CAP, PW), BF),
            pltpu.VMEM((NS, 1, 128), F32),
            pltpu.VMEM((NS, 1, 128), F32),
            pltpu.VMEM((1, D), F32),
            pltpu.VMEM((ND, 1, D), F32),
            pltpu.VMEM((NY, NX, ROWS_DP, FQ), BF),
            pltpu.VMEM((NX, FF_DP, D), BF),
            pltpu.VMEM((2, NY, TOK, D), BF),
            pltpu.VMEM((2, NY * TOK, FQ), BF),
            pltpu.VMEM((NY * TOK, FQ), F32),
            pltpu.VMEM((NY * TOK, FQ), F32),
            pltpu.VMEM((NY, TOK, D), BF),
            pltpu.VMEM((NY, TOK, D), BF),
            pltpu.VMEM((2, FQ, D), BF),
            pltpu.VMEM((FQ, D), BF),
            pltpu.VMEM((FQ, D), BF),
            pltpu.VMEM((NX, FF_DP, D), BF),
            pltpu.VMEM((FF_DP, D), BF),
            pltpu.VMEM((NZ, FF_DP, WIN), BF),
            pltpu.VMEM((FF_DP, WIN), BF),
            pltpu.VMEM((FF_DP, WIN), BF),
            pltpu.VMEM((FF_DP, WIN), BF),
            pltpu.VMEM((1, D), F32),
            pltpu.VMEM((NS, 1, D), F32),
            pltpu.VMEM((1, D), F32),
            pltpu.VMEM((ND, 1, D), F32),
            pltpu.VMEM((HEADS, TOK, TOK), F32),
            pltpu.VMEM((TOK, D), BF),
            pltpu.VMEM((TOK, D), F32),
            pltpu.VMEM((TOK, 1), F32),
            *sems,
        ],
        compiler_params=pltpu.CompilerParams(
            collective_id=0, has_side_effects=True, vmem_limit_bytes=56 * 2**20
        ),
    )(*args)


def hand_out_kernel(*refs):
    n = 7
    ins, outs, held = refs[:n], refs[n : 2 * n], refs[2 * n : 3 * n]
    flat, taken, done = refs[3 * n :]
    into = [pltpu.make_async_copy(ins[i], held[i], taken.at[i]) for i in range(n)]
    out = [
        pltpu.make_async_copy(held[i] if i < n - 1 else flat, outs[i], done.at[i])
        for i in range(n)
    ]
    for copy in into:
        copy.start()
    for i in range(n):
        into[i].wait()
        if i == n - 1:
            flat[...] = held[i][0, :]
        out[i].start()
    for copy in out:
        copy.wait()


def hand_out(arrays):
    hbm = pl.BlockSpec(memory_space=pl.ANY)
    return pl.pallas_call(
        hand_out_kernel,
        out_shape=tuple(jax.ShapeDtypeStruct(a.shape, a.dtype) for a in arrays[:-1])
        + (jax.ShapeDtypeStruct((D,), F32),),
        in_specs=[hbm] * 7,
        out_specs=(hbm,) * 7,
        scratch_shapes=[
            *[pltpu.VMEM(a.shape, a.dtype) for a in arrays],
            pltpu.VMEM((D,), F32),
            pltpu.SemaphoreType.DMA((7,)),
            pltpu.SemaphoreType.DMA((7,)),
        ],
    )(*arrays)


def per_device(
    queries, key_rows, value_rows, resid_in, llm_grad, vision_slot, window_mask, w_up, w_down,
    norm_gain,
):
    results = layer(
        queries[0],
        key_rows[0],
        value_rows[0],
        resid_in[0],
        llm_grad[0],
        vision_slot,
        window_mask,
        w_up,
        w_down,
        norm_gain.reshape(1, ROWS_DP),
    )
    grad_query, grad_key, grad_value, grad_resid, grad_up, grad_down, grad_gain = hand_out(results)
    return (
        grad_query[None],
        grad_key[None],
        grad_value[None],
        grad_resid[None],
        grad_up,
        grad_down,
        grad_gain,
    )


def solution(mesh):
    row3 = P("dp", "seq", None)
    in_specs = (
        row3,
        row3,
        row3,
        row3,
        row3,
        P("dp", "seq"),
        row3,
        P("dp", None),
        P("dp", None),
        P("dp"),
    )
    out_specs = (row3, row3, row3, row3, P("seq", "dp"), P("seq", "dp"), P())
    return jax.shard_map(
        per_device, mesh=mesh, in_specs=in_specs, out_specs=out_specs, check_vma=False
    )
```

```python
import math

import jax
import jax.numpy as jnp
from jax import lax
from jax.experimental import pallas as pl
from jax.experimental.pallas import tpu as pltpu
from jax.sharding import PartitionSpec as P

HEADS = 16
HDIM = 80
BLK = 64
D = 1280
FF = 2560
TOK = 128
POS = 192
NS = 16
ND = 16
CAP = 32
NY, NX, NZ = 4, 4, 8
FQ = FF // NY
ROWS_DP = D // ND
FF_DP = FF // ND
WIN = 256
NP = 5
PW = D // NP
NR = 5
RW = FF_DP // NR
MESH = pl.DeviceIdType.MESH
BF = jnp.bfloat16
F32 = jnp.float32


def mm(left, right, left_dim, right_dim):
    return lax.dot_general(
        left, right, (((left_dim,), (right_dim,)), ((), ())), preferred_element_type=F32
    )


def iota(shape, dim):
    return lax.broadcasted_iota(jnp.int32, shape, dim)


def to_column(row):
    n = row.shape[1]
    same = iota((n, n), 0) == iota((n, n), 1)
    return jnp.sum(jnp.where(same, row, 0.0), axis=1, keepdims=True)


def window_start(z):
    return pl.multiple_of(128 * ((5 * z) // 4), 128)


SEMS = {
    "gr": ND, "rr": NP * NS, "ri": NS, "wy": NY, "wx": NX, "rl": NX, "na": NY, "nf": 2, "ga": NP * NY, "gf": NP * 2,
    "dn": NY, "c": 5, "x": NR * NX, "z": NR * NZ, "f": 3, "g1": NS, "g2": ND,
}


def kernel(
    q_hbm, k_hbm, v_hbm, resid_hbm, llm_hbm, slot_ref, mask_ref, wup_ref, wdown_ref, ngain_ref,
    gq_hbm, gk_hbm, gv_hbm, gresid_hbm, up_ref, down_ref, ggain_ref,
    q_ref, k_ref, v_ref, resid_ref, llm_ref, gq_ref, gk_ref, gv_ref, gresid_ref,
    rs, rr, ids, ri, gsh, gr, wu, wd, ra, la, gate, dact, dns, dnr, gt, cr, xs, xr, zs, zr,
    fs, fu, fd, gp, gs1, gp2, gs2, probs, att, unit, inv, s_loc, *sems,
):
    names = list(SEMS)
    send = {n: sems[2 * i] for i, n in enumerate(names)}
    recv = {n: sems[2 * i + 1] for i, n in enumerate(names)}
    s = lax.axis_index("seq")
    d = lax.axis_index("dp")
    z, c = s // 2, s % 2
    y, x = d // NX, d % NX
    scale = 1.0 / math.sqrt(HDIM)

    def remote(src, dst, name, at, to_s, to_d, at_recv=None):
        return pltpu.make_async_remote_copy(
            src_ref=src,
            dst_ref=dst,
            send_sem=send[name].at[at],
            recv_sem=recv[name].at[at if at_recv is None else at_recv],
            device_id=(to_s, to_d),
            device_id_type=MESH,
        )

    def y_peer(k):
        return ((y + k) % NY) * NX + x

    def x_peer(k):
        return y * NX + (x + k) % NX

    def local(src, dst, at):
        return pltpu.make_async_copy(src, dst, s_loc.at[at])

    loads = [
        local(llm_hbm, llm_ref, 3),
        local(q_hbm, q_ref, 4),
        local(k_hbm, k_ref, 5),
        local(v_hbm, v_ref, 6),
        local(resid_hbm, resid_ref, 7),
    ]
    stores = [
        local(gresid_ref, gresid_hbm, 8),
        local(gq_ref, gq_hbm, 9),
        local(gk_ref, gk_hbm, 10),
        local(gv_ref, gv_hbm, 11),
    ]
    for copy in loads:
        copy.start()

    barrier = pltpu.get_barrier_semaphore()
    for k in range(1, NS):
        pl.semaphore_signal(barrier, inc=1, device_id=((s + k) % NS, d), device_id_type=MESH)
    for k in range(1, ND):
        pl.semaphore_signal(barrier, inc=1, device_id=(s, (d + k) % ND), device_id_type=MESH)
    from_s = 2 * (d // 2) + 1
    own_final = jnp.logical_and(from_s == s, s == d)

    @pl.when(jnp.logical_not(own_final))
    def _():
        pl.semaphore_signal(barrier, inc=1, device_id=(from_s, s), device_id_type=MESH)

    slot_row = slot_ref[...].astype(F32)
    slot_col = to_column(slot_row)
    owner_row = jnp.floor(slot_row * (1.0 / TOK))
    owner_col = jnp.floor(slot_col * (1.0 / TOK))
    at0, at1 = iota((POS, POS), 0), iota((POS, POS), 1)
    same = owner_col == owner_row
    rank_row = jnp.sum(jnp.where(same & (at0 < at1), 1.0, 0.0), axis=0, keepdims=True)
    rank_col = jnp.sum(jnp.where(same & (at1 < at0), 1.0, 0.0), axis=1, keepdims=True)
    target_row = jnp.where(slot_row >= 0.0, owner_row * CAP + rank_row, -1.0)
    target_col = jnp.where(slot_col >= 0.0, owner_col * CAP + rank_col, -1.0)
    hit = iota((NS * CAP, POS), 0).astype(F32) == target_row
    pick = jnp.where(hit, 1.0, 0.0).astype(BF)
    loads[0].wait()
    for p in range(NP):
        rs[p] = mm(pick, llm_ref[:, PW * p : PW * p + PW], 1, 0).astype(BF).reshape(NS, CAP, PW)
    lane = iota((1, 128), 1)
    lane_slot = (lane % CAP).astype(F32)
    mine = lane // CAP == s % 4
    landing = slot_col - owner_col * TOK + 1.0
    for o in range(NS):
        found = jnp.where((target_col == lane_slot + float(o * CAP)) & mine, landing, 0.0)
        ids[o] = jnp.sum(found, axis=0, keepdims=True) - 1.0
    ngain_col = to_column(ngain_ref[...].astype(F32))
    place_gain = iota((ROWS_DP, D), 1) == iota((ROWS_DP, D), 0) + d * ROWS_DP
    gsh[...] = jnp.sum(jnp.where(place_gain, ngain_col, 0.0), axis=0, keepdims=True)

    pl.semaphore_wait(barrier, NS + ND - 2 + 2 * c - jnp.where(own_final, 1, 0))

    def gain_copy(k):
        return remote(gsh, gr.at[d], "gr", k, s, (d + k) % ND)

    def row_copy(p, k):
        to = (s + k) % NS
        return remote(rs.at[p, to], rr.at[p, s], "rr", p * NS + k, to, d)

    def id_copy(k):
        to = (s + k) % NS
        return remote(ids.at[to], ri.at[s], "ri", k, to, d)

    far_first = (8, 7, 9, 6, 10, 5, 11, 4, 12, 3, 13, 2, 14, 1, 15)
    for k in far_first:
        id_copy(k).start()
    for k in far_first:
        row_copy(0, k).start()
    for k in range(1, ND):
        gain_copy(k).start()

    def quarter(q):
        return wup_ref.at[:, pl.ds(pl.multiple_of(q * FQ, 128), FQ)]

    def wy_copy(k):
        return remote(quarter((y + k) % NY), wu.at[y, x], "wy", k, s, y_peer(k))

    def ux_copy(k):
        return remote(wu.at[:, x], wu.at[:, x], "wx", k, s, x_peer(k))

    def dx_copy(k):
        return remote(wd.at[x], wd.at[x], "wx", k, s, x_peer(k))

    def ul_copy(k):
        at = (x + NX - k) % NX
        return remote(wu.at[:, at], wu.at[:, at], "rl", k, s + 1, d)

    def dl_copy(k):
        at = (x + NX - k) % NX
        return remote(wd.at[at], wd.at[at], "rl", k, s - 1, d)

    own_up = pltpu.make_async_copy(quarter(y), wu.at[y, x], s_loc.at[0])
    own_down = pltpu.make_async_copy(wdown_ref, wd.at[x], s_loc.at[1])

    @pl.when(c == 0)
    def _():
        for k in (2, 1, 3):
            wy_copy(k).start()
        own_up.start()
        own_up.wait()

    @pl.when(c == 1)
    def _():
        own_down.start()
        own_down.wait()
        for k in (2, 1, 3):
            dx_copy(k).start()
        dl_copy(0).start()

    for p in range(1, NP):
        for k in far_first:
            row_copy(p, k).start()
    for p in range(NP):
        rr[p, s] = rs[p, s]
    ri[s] = ids[s]

    row_late = iota((TOK, TOK), 0) >= BLK
    col_late = iota((TOK, TOK), 1) >= BLK
    flags = [[mask_ref[0, i : i + 1, j : j + 1] for j in range(2)] for i in range(2)]
    allowed = (
        jnp.where(
            row_late,
            jnp.where(col_late, flags[1][1], flags[1][0]),
            jnp.where(col_late, flags[0][1], flags[0][0]),
        )
        > 0
    )

    def window(h):
        first, last = HDIM * h // 128, (HDIM * h + HDIM - 1) // 128
        lanes = slice(128 * first, 128 * last + 128)
        feature = iota((1, lanes.stop - lanes.start), 1) + lanes.start
        inside = (feature >= HDIM * h) & (feature < HDIM * h + HDIM)
        return lanes, jnp.where(inside, 1.0, 0.0).astype(BF)

    class Tiles:
        def __init__(self, out):
            self.out, self.open = out, {}

        def add(self, h, value):
            first = HDIM * h // 128
            for i in range(value.shape[1] // 128):
                part = value[:, 128 * i : 128 * i + 128]
                held = self.open.get(first + i)
                self.open[first + i] = part if held is None else held + part
            upto = HDIM * (h + 1) // 128 if h + 1 < HEADS else D // 128
            for t in [t for t in self.open if t < upto]:
                self.out[:, 128 * t : 128 * t + 128] = self.open.pop(t).astype(BF)

    att_tiles = Tiles(att)

    def attend(h):
        lanes, inside = window(h)
        scores = mm(q_ref[:, lanes], k_ref[:, lanes] * inside, 1, 1) * scale
        masked = jnp.where(allowed, scores, -jnp.inf)
        highest = jnp.max(masked, axis=1, keepdims=True)
        terms = jnp.where(allowed, jnp.exp(masked - highest), 0.0)
        prob = terms * (1.0 / jnp.sum(terms, axis=1, keepdims=True))
        probs[h] = prob
        att_tiles.add(h, mm(prob.astype(BF), v_ref[:, lanes] * inside, 1, 0))

    for copy in loads[1:]:
        copy.wait()
    for h in range(HEADS // 2):
        attend(h)

    @pl.when(c == 0)
    def _():
        for k in range(1, NY):
            wy_copy(k).wait_recv()
        for k in (2, 1, 3):
            ux_copy(k).start()
        ul_copy(0).start()

    for h in range(HEADS // 2, HEADS):
        attend(h)

    gr[d] = gsh[...]
    for k in range(1, ND):
        gain_copy(k).wait_recv()
    gain_full = jnp.sum(gr[...], axis=0)

    def unit_step(i, carry):
        rows = pl.ds(pl.multiple_of(i * 32, 32), 32)
        hidden = resid_ref[rows, :].astype(F32) + att[rows, :].astype(F32)
        center = jnp.mean(hidden, axis=1, keepdims=True)
        away = hidden - center
        inverse = lax.rsqrt(jnp.mean(away * away, axis=1, keepdims=True) + 1e-06)
        inv[rows, :] = inverse
        out = away * inverse
        unit[rows, :] = out
        ra[0, y, rows, :] = (out * gain_full).astype(BF)
        return carry

    lax.fori_loop(0, TOK // 32, unit_step, 0)

    def na_copy(k):
        return remote(ra.at[0, y], ra.at[0, y], "na", k, s, y_peer(k))

    for k in (1, 3):
        na_copy(k).start()

    def nf_copy(way):
        at = (y + NY - 1) % NY if way == 0 else (y + 1) % NY
        view = ra.at[0, at, pl.ds(way * BLK, BLK)]
        return remote(view, view, "nf", way, s, y_peer(1 if way == 0 else 3))

    def n_forward():
        for way, k in ((0, 1), (1, 3)):
            na_copy(k).wait_recv()
            nf_copy(way).start()

    @pl.when(c == 1)
    def _():
        for k in (1, 3, 2):
            dx_copy(k).wait_recv()
            dl_copy(k).start()

    for k in range(1, NS):
        id_copy(k).wait_recv()
    token = iota((TOK, 128), 0).astype(F32)
    place = jnp.concatenate(
        [
            jnp.where(token == jnp.max(ri[4 * j : 4 * j + 4], axis=0), 1.0, 0.0).astype(BF)
            for j in range(4)
        ],
        axis=1,
    )

    def piece(p):
        return slice(PW * p, PW * p + PW)

    def ga_copy(p, k):
        view = ra.at[1, y, :, piece(p)]
        return remote(view, view, "ga", p * NY + k, s, y_peer(k))

    def gf_copy(p, way):
        at = (y + NY - 1) % NY if way == 0 else (y + 1) % NY
        view = ra.at[1, at, pl.ds(way * BLK, BLK), piece(p)]
        return remote(view, view, "gf", p * 2 + way, s, y_peer(1 if way == 0 else 3))

    def rows_in(p):
        for k in range(1, NS):
            row_copy(p, k).wait_recv()
        ra[1, y, :, piece(p)] = mm(place, rr[p].reshape(NS * CAP, PW), 1, 0).astype(BF)
        for k in (1, 3) if p < NP - 1 else (2, 1, 3):
            ga_copy(p, k).start()
        if p > 0:
            for way, k in ((0, 1), (1, 3)):
                ga_copy(p - 1, k).wait_recv()
                gf_copy(p - 1, way).start()

    rows_in(0)
    rows_in(1)
    n_forward()
    rows_in(2)

    @pl.when(c == 0)
    def _():
        for k in (1, 3, 2):
            ux_copy(k).wait_recv()
            ul_copy(k).start()

    @pl.when(c == 1)
    def _():
        for k in range(NX):
            ul_copy(k).wait_recv()

    for way in range(2):
        nf_copy(way).wait_recv()
    half = 2 * TOK

    def up_step(i, carry):
        rows = pl.ds(pl.multiple_of(i * half, half), half)
        pre = mm(ra[0, pl.ds(2 * i, 2)].reshape(half, D), wu[...].reshape(D, FQ), 1, 0)
        sig = jax.nn.sigmoid(1.702 * pre)
        la[1, rows, :] = (pre * sig).astype(BF)
        gate[rows, :] = sig + 1.702 * pre * sig * (1.0 - sig)
        return carry

    lax.fori_loop(0, 2, up_step, 0)

    rows_in(3)
    rows_in(4)

    @pl.when(c == 0)
    def _():
        for k in range(NX):
            dl_copy(k).wait_recv()

    def cd_copy(p):
        return remote(gt.at[1, :, piece(p)], cr.at[:, piece(p)], "c", p, s + 1, d)

    def cu_copy(i):
        rows = slice(128 * i, 128 * i + 128)
        return remote(gt.at[0, rows], cr.at[rows], "c", i, s - 1, d)

    def down_in(p):
        cd_copy(p).wait_recv()
        xs[:, piece(p)] = (
            gt[1, :, piece(p)].astype(F32) + cr[:, piece(p)].astype(F32)
        ).astype(BF)

    for k in range(1, NS):
        for p in range(NP):
            row_copy(p, k).wait_send()
        id_copy(k).wait_send()
    for k in range(1, ND):
        gain_copy(k).wait_send()

    for p in range(NP):
        if p < NP - 1:
            for way in range(2):
                gf_copy(p, way).wait_recv()
        else:
            for k in range(1, NY):
                ga_copy(p, k).wait_recv()
        grads = ra[1, :, :, piece(p)].reshape(NY * TOK, PW)
        part = mm(grads, wd[:, :, piece(p)].reshape(FQ, PW), 1, 1)
        dact[...] = part if p == 0 else dact[...] + part
        gt[1, :, piece(p)] = mm(la[1], grads, 0, 0).astype(BF)

        @pl.when(c == 0)
        def _(p=p):
            cd_copy(p).start()

        if p > 0:

            @pl.when(c == 1)
            def _(p=p):
                down_in(p - 1)

    la[0] = (dact[...] * gate[...]).astype(BF)

    def x_copy(r, k):
        to = (x + k) % NX
        rows = pl.ds(pl.multiple_of(to * FF_DP + r * RW, RW), RW)
        return remote(
            xs.at[rows], xr.at[x, pl.ds(r * RW, RW)], "x", r * NX + k, s, y * NX + to
        )

    @pl.when(c == 1)
    def _():
        down_in(NP - 1)
        for r in range(NR):
            for k in (2, 1, 3):
                x_copy(r, k).start()

    def norm_step(i, acc):
        rows = pl.ds(pl.multiple_of(i * half, half), half)
        part = mm(la[0, rows, :], wu[...].reshape(D, FQ), 1, 1)
        dns[pl.ds(2 * i, 2)] = part.astype(BF).reshape(2, TOK, D)
        normed = ra[0, pl.ds(2 * i, 2)].reshape(half, D).astype(F32)
        return acc + jnp.sum(part * normed, axis=0, keepdims=True)

    gp[...] = lax.fori_loop(0, 2, norm_step, jnp.zeros((1, D), F32))

    def dn_copy(k):
        to = (y + k) % NY
        return remote(dns.at[to], dnr.at[y], "dn", k, s, to * NX + x)

    for k in (2, 1, 3):
        dn_copy(k).start()

    def g1_copy(k):
        return remote(gp, gs1.at[s], "g1", k, (s + k) % NS, d)

    for k in range(1, NS):
        g1_copy(k).start()

    for i in range(FQ // 128):
        rows = slice(128 * i, 128 * i + 128)
        gt[0, rows, :] = mm(la[0, :, rows], ra[0].reshape(NY * TOK, D), 0, 0).astype(BF)

        @pl.when(c == 1)
        def _(i=i):
            cu_copy(i).start()

    @pl.when(c == 0)
    def _():
        for i in range(FQ // 128):
            cu_copy(i).wait_recv()
        for r in range(NR):
            for b in range(NX):
                rows = pl.ds(b * FF_DP + r * RW, RW)
                xs[rows, :] = (gt[0, rows, :].astype(F32) + cr[rows, :].astype(F32)).astype(BF)
            for k in (2, 1, 3):
                x_copy(r, k).start()

    def z_copy(r, k):
        to = (z + k) % NZ
        rows = pl.ds(r * RW, RW)
        return remote(
            zs.at[rows, pl.ds(window_start(to), WIN)],
            zr.at[z, rows],
            "z",
            r * NZ + k,
            2 * to + c,
            d,
        )

    for r in range(NR):
        rows = pl.ds(r * RW, RW)
        own = pl.ds(pl.multiple_of(x * FF_DP + r * RW, RW), RW)
        for k in range(1, NX):
            x_copy(r, k).wait_recv()
        xr[x, rows] = xs[own, :]
        zs[rows, :] = jnp.sum(xr[:, rows, :].astype(F32), axis=0).astype(BF)
        for k in (4, 3, 5, 2, 6, 1, 7):
            z_copy(r, k).start()
        zr[z, rows] = zs[rows, pl.ds(window_start(z), WIN)]

    gs1[s] = gp[...]
    for k in range(1, NS):
        g1_copy(k).wait_recv()
    gp2[...] = jnp.sum(gs1[...], axis=0)

    def g2_copy(k):
        return remote(gp2, gs2.at[d], "g2", k, s, (d + k) % ND)

    for k in range(1, ND):
        g2_copy(k).start()

    dnr[y] = dns[y]
    for k in range(1, NY):
        dn_copy(k).wait_recv()
    gain_again = jnp.sum(gr[...], axis=0)

    def resid_step(i, carry):
        rows = pl.ds(pl.multiple_of(i * 32, 32), 32)
        d_unit = jnp.sum(dnr[:, rows, :].astype(F32), axis=0) * gain_again
        normal = unit[rows, :]
        first = jnp.mean(d_unit, axis=1, keepdims=True)
        second = jnp.mean(d_unit * normal, axis=1, keepdims=True)
        d_hidden = inv[rows, :] * (d_unit - first - normal * second)
        gresid_ref[rows, :] = (ra[1, y, rows, :].astype(F32) + d_hidden).astype(BF)
        return carry

    lax.fori_loop(0, TOK // 32, resid_step, 0)

    stores[0].start()
    gq_tiles, gk_tiles, gv_tiles = Tiles(gq_ref), Tiles(gk_ref), Tiles(gv_ref)
    for h in range(HEADS):
        lanes, inside = window(h)
        grad = gresid_ref[:, lanes] * inside
        prob = probs[h]
        gv_tiles.add(h, mm(prob.astype(BF), grad, 0, 0))
        d_probs = mm(grad, v_ref[:, lanes], 1, 1)
        delta = jnp.sum(
            grad.astype(F32) * att[:, lanes].astype(F32), axis=1, keepdims=True
        )
        d_scores = (prob * (d_probs - delta) * scale).astype(BF)
        gq_tiles.add(h, mm(d_scores, k_ref[:, lanes] * inside, 1, 0))
        gk_tiles.add(h, mm(d_scores, q_ref[:, lanes] * inside, 0, 0))
    for copy in stores[1:]:
        copy.start()

    factor = 1.0 / math.sqrt(NS * ND * TOK)
    gs2[d] = gp2[...]
    for k in range(1, ND):
        g2_copy(k).wait_recv()
    ggain_ref[...] = jnp.sum(gs2[...], axis=0) * factor / gain_again

    for r in range(NR):
        for k in range(1, NZ):
            z_copy(r, k).wait_recv()
    fs[...] = (jnp.sum(zr[...].astype(F32), axis=0) * factor).astype(BF)

    u_copy = remote(fs, fu, "f", 0, s + 1, d)
    d0_copy = remote(fs, fd, "f", 1, d, 2 * z)
    d1_copy = remote(fs, fd, "f", 2, d, 2 * z + 1, 1)
    own_down_out = pltpu.make_async_copy(fs, fd, s_loc.at[2])

    def chosen(first):
        return jnp.where(
            iota((ROWS_DP, WIN), 1) == iota((ROWS_DP, WIN), 0) + first, 1.0, 0.0
        ).astype(BF)

    own_lanes = chosen(32 * (z % 4) + ROWS_DP * c)

    @pl.when(c == 0)
    def _():
        u_copy.start()
        up_ref[...] = mm(own_lanes, fs[...], 1, 1).astype(BF)

    @pl.when(c == 1)
    def _():
        d0_copy.start()

        @pl.when(s == d)
        def _():
            own_down_out.start()
            own_down_out.wait()

        @pl.when(s != d)
        def _():
            d1_copy.start()

        u_copy.wait_recv()
        up_ref[...] = mm(own_lanes, fu[...], 1, 1).astype(BF)

    @pl.when(jnp.logical_not(own_final))
    def _():
        d0_copy.wait_recv()

    down_ref[...] = mm(
        fd[...], chosen(32 * ((d // 2) % 4) + ROWS_DP * (d % 2)), 1, 1
    ).astype(BF)

    @pl.when(c == 0)
    def _():
        u_copy.wait_send()
        for k in range(1, NY):
            wy_copy(k).wait_send()
        for k in range(1, NX):
            ux_copy(k).wait_send()
        for k in range(NX):
            ul_copy(k).wait_send()
        for p in range(NP):
            cd_copy(p).wait_send()

    @pl.when(c == 1)
    def _():
        d0_copy.wait_send()

        @pl.when(s != d)
        def _():
            d1_copy.wait_send()

        for k in range(1, NX):
            dx_copy(k).wait_send()
        for k in range(NX):
            dl_copy(k).wait_send()
        for i in range(FQ // 128):
            cu_copy(i).wait_send()

    for k in range(1, NS):
        g1_copy(k).wait_send()
    for k in range(1, ND):
        g2_copy(k).wait_send()
    for k in range(1, NY):
        if k != 2:
            na_copy(k).wait_send()
        for p in range(NP):
            if k != 2 or p == NP - 1:
                ga_copy(p, k).wait_send()
        dn_copy(k).wait_send()
    for way in range(2):
        nf_copy(way).wait_send()
        for p in range(NP - 1):
            gf_copy(p, way).wait_send()
    for copy in stores:
        copy.wait()
    for r in range(NR):
        for k in range(1, NX):
            x_copy(r, k).wait_send()
        for k in range(1, NZ):
            z_copy(r, k).wait_send()


def layer(*args):
    vm = pl.BlockSpec(memory_space=pltpu.VMEM)
    hbm = pl.BlockSpec(memory_space=pl.ANY)
    sem = pltpu.SemaphoreType.DMA
    sems = [sem((12,))]
    for n in SEMS.values():
        sems += [sem((n,)), sem((n,))]
    out = jax.ShapeDtypeStruct
    return pl.pallas_call(
        kernel,
        out_shape=(
            out((TOK, D), BF),
            out((TOK, D), BF),
            out((TOK, D), BF),
            out((TOK, D), BF),
            out((ROWS_DP, FF_DP), BF),
            out((FF_DP, ROWS_DP), BF),
            out((1, D), F32),
        ),
        in_specs=[hbm] * 5 + [vm, vm, hbm, hbm, vm],
        out_specs=(hbm,) * 4 + (vm,) * 3,
        scratch_shapes=[
            *[pltpu.VMEM((TOK, D), BF)] * 4,
            pltpu.VMEM((POS, D), BF),
            *[pltpu.VMEM((TOK, D), BF)] * 4,
            pltpu.VMEM((NP, NS, CAP, PW), BF),
            pltpu.VMEM((NP, NS, CAP, PW), BF),
            pltpu.VMEM((NS, 1, 128), F32),
            pltpu.VMEM((NS, 1, 128), F32),
            pltpu.VMEM((1, D), F32),
            pltpu.VMEM((ND, 1, D), F32),
            pltpu.VMEM((NY, NX, ROWS_DP, FQ), BF),
            pltpu.VMEM((NX, FF_DP, D), BF),
            pltpu.VMEM((2, NY, TOK, D), BF),
            pltpu.VMEM((2, NY * TOK, FQ), BF),
            pltpu.VMEM((NY * TOK, FQ), F32),
            pltpu.VMEM((NY * TOK, FQ), F32),
            pltpu.VMEM((NY, TOK, D), BF),
            pltpu.VMEM((NY, TOK, D), BF),
            pltpu.VMEM((2, FQ, D), BF),
            pltpu.VMEM((FQ, D), BF),
            pltpu.VMEM((FQ, D), BF),
            pltpu.VMEM((NX, FF_DP, D), BF),
            pltpu.VMEM((FF_DP, D), BF),
            pltpu.VMEM((NZ, FF_DP, WIN), BF),
            pltpu.VMEM((FF_DP, WIN), BF),
            pltpu.VMEM((FF_DP, WIN), BF),
            pltpu.VMEM((FF_DP, WIN), BF),
            pltpu.VMEM((1, D), F32),
            pltpu.VMEM((NS, 1, D), F32),
            pltpu.VMEM((1, D), F32),
            pltpu.VMEM((ND, 1, D), F32),
            pltpu.VMEM((HEADS, TOK, TOK), F32),
            pltpu.VMEM((TOK, D), BF),
            pltpu.VMEM((TOK, D), F32),
            pltpu.VMEM((TOK, 1), F32),
            *sems,
        ],
        compiler_params=pltpu.CompilerParams(
            collective_id=0, has_side_effects=True, vmem_limit_bytes=56 * 2**20
        ),
    )(*args)


def hand_out_kernel(*refs):
    n = 7
    ins, outs, held = refs[:n], refs[n : 2 * n], refs[2 * n : 3 * n]
    flat, taken, done = refs[3 * n :]
    into = [pltpu.make_async_copy(ins[i], held[i], taken.at[i]) for i in range(n)]
    out = [
        pltpu.make_async_copy(held[i] if i < n - 1 else flat, outs[i], done.at[i])
        for i in range(n)
    ]
    for copy in into:
        copy.start()
    for i in range(n):
        into[i].wait()
        if i == n - 1:
            flat[...] = held[i][0, :]
        out[i].start()
    for copy in out:
        copy.wait()


def hand_out(arrays):
    hbm = pl.BlockSpec(memory_space=pl.ANY)
    return pl.pallas_call(
        hand_out_kernel,
        out_shape=tuple(jax.ShapeDtypeStruct(a.shape, a.dtype) for a in arrays[:-1])
        + (jax.ShapeDtypeStruct((D,), F32),),
        in_specs=[hbm] * 7,
        out_specs=(hbm,) * 7,
        scratch_shapes=[
            *[pltpu.VMEM(a.shape, a.dtype) for a in arrays],
            pltpu.VMEM((D,), F32),
            pltpu.SemaphoreType.DMA((7,)),
            pltpu.SemaphoreType.DMA((7,)),
        ],
    )(*arrays)


def per_device(
    queries, key_rows, value_rows, resid_in, llm_grad, vision_slot, window_mask, w_up, w_down,
    norm_gain,
):
    results = layer(
        queries[0],
        key_rows[0],
        value_rows[0],
        resid_in[0],
        llm_grad[0],
        vision_slot,
        window_mask,
        w_up,
        w_down,
        norm_gain.reshape(1, ROWS_DP),
    )
    grad_query, grad_key, grad_value, grad_resid, grad_up, grad_down, grad_gain = hand_out(results)
    return (
        grad_query[None],
        grad_key[None],
        grad_value[None],
        grad_resid[None],
        grad_up,
        grad_down,
        grad_gain,
    )


def solution(mesh):
    row3 = P("dp", "seq", None)
    in_specs = (
        row3,
        row3,
        row3,
        row3,
        row3,
        P("dp", "seq"),
        row3,
        P("dp", None),
        P("dp", None),
        P("dp"),
    )
    out_specs = (row3, row3, row3, row3, P("seq", "dp"), P("seq", "dp"), P())
    return jax.shard_map(
        per_device, mesh=mesh, in_specs=in_specs, out_specs=out_specs, check_vma=False
    )
```
